256 devices in a mesh: blk: 32 (over z, y_lo, core), head: 8 (over y_hi, x).
Axes of the slice: x: 4, y: 4 (y_hi: 2, y_lo: 2; y = y_hi * 2 + y_lo), z: 8, core: 2. Of those that a mesh axis runs over, the one named last changes fastest.
Arguments:
- hidden: bfloat16 [2048, 5120], P('blk'), may hold values from -6 to 6
- norm_gain: float32 [5120], replicated, may hold values from 0.1 to 1.9
- w_query: bfloat16 [5120, 5120], P('blk', 'head'), may hold values from -0.078125 to 0.078125
- key_projection_weight: bfloat16 [5120, 1024], P('blk', 'head'), may hold values from -0.3125 to 0.3125
- value_projection_weight: bfloat16 [5120, 1024], P('blk', 'head'), may hold values from -0.078125 to 0.078125
- w_out: bfloat16 [5120, 5120], P('head', 'blk'), may hold values from -0.078125 to 0.078125
- cache_keys: bfloat16 [8, 65536, 128], P('head', 'blk'), may hold values from -1024 to 1024
- earlier_values: bfloat16 [8, 65536, 128], P('head', 'blk'), may hold values from -6 to 6
- cache_len: int32 [32], P('blk'), may hold values from 512 to 2048, as said below
- stretch_start: int32 [1], replicated, may hold values from 0 to 4194303
Outputs:
- attention_out: bfloat16 [2048, 5120], P('head', 'blk')
The draws below stay inside these ranges and needn't reach their ends.
Inputs may be any that keep to these rules, and one draw needn't show every extreme that they name: Cache shard s holds valid entries at its first cache_len[s] positions, the rest are ignored; at least one shard is full.
All inputs are finite; a program needn't handle non-finite values.
Results may differ from the reference program's by a relative error of at most 0.023.
The reference program's roundings to bfloat16 on the way count: a program that leaves them out, or rounds other values in their place, can miss the bound.
Values may be sent and summed in bfloat16 or wider, within the bound.
No kernel may reach another device: no remote copies, remote signals or barrier semaphores. Data moves between devices by JAX's collectives and lax.ppermute only.
A program may use at most 192 MiB of HBM per device.

```python
import jax
import jax.numpy as jnp
from jax import lax

MODEL_DIMENSION = 5120
QUERY_HEADS = 40
KEY_VALUE_HEADS = 8
HEAD_SIZE = 128
CACHE_DEV = 2048
STRETCH_TOKENS = 2048
CACHE_POSITIONS = 65536
CACHE_SHARDS = 32
N_BLK = 32


def draw_cache_keys(key, part):
    table_entries = 3.0 * jnp.clip(jax.random.normal(key, (KEY_VALUE_HEADS, CACHE_POSITIONS, HEAD_SIZE), jnp.float32), -4.0, 4.0)
    return table_entries.astype(jnp.bfloat16)


def draw_cache_len(key, part):
    lengths = jax.random.randint(key, (CACHE_SHARDS,), CACHE_DEV // 4, CACHE_DEV + 1)
    full_shard = jax.random.randint(jax.random.fold_in(key, 7), (), 0, CACHE_SHARDS)
    return lengths.at[full_shard].set(CACHE_DEV).astype(jnp.int32)


def block_levels(rng, shape, shards, low, top_value):
    def one(dim, blocks):
        heights = jax.random.uniform(jax.random.fold_in(jax.random.fold_in(rng, 6), dim), (blocks,), jnp.float32, low / len(shards), top_value / len(shards))
        return jnp.repeat(jnp.exp(heights), shape[dim] // blocks).reshape((-1,) + (1,) * (len(shape) - dim - 1))

    loudness = one(*shards[0])
    for cut in shards[1:]:
        loudness = loudness * one(*cut)
    return loudness


def scatter_about(rng, extent, width, most, pieces=(), held_as=jnp.bfloat16):
    loudness = block_levels(rng, extent, pieces, -0.22, 0.18) if pieces else 1.0
    drawn = jax.random.normal(rng, extent, jnp.float32) * width * loudness
    return jnp.minimum(jnp.maximum(drawn, -most), most).astype(held_as)


def setup_inputs(seed: int = 0) -> dict:
    key_list = jax.random.split(jax.random.key(seed), 11)
    return {
        "hidden": scatter_about(key_list[0], (STRETCH_TOKENS, MODEL_DIMENSION), 1.0, 6.0, ((0, 32),)),
        "norm_gain": jnp.clip(1.0 + 0.18 * jax.random.normal(key_list[1], (MODEL_DIMENSION,), jnp.float32), 0.1, 1.9),
        "w_query": scatter_about(key_list[2], (MODEL_DIMENSION, QUERY_HEADS * HEAD_SIZE), MODEL_DIMENSION ** -0.5, 0.078125, ((0, 32), (1, 8))),
        "key_projection_weight": scatter_about(key_list[3], (MODEL_DIMENSION, KEY_VALUE_HEADS * HEAD_SIZE), (MODEL_DIMENSION // 16) ** -0.5, 0.3125, ((0, 32), (1, 8))),
        "value_projection_weight": scatter_about(key_list[4], (MODEL_DIMENSION, KEY_VALUE_HEADS * HEAD_SIZE), MODEL_DIMENSION ** -0.5, 0.078125, ((0, 32), (1, 8))),
        "w_out": scatter_about(key_list[5], (QUERY_HEADS * HEAD_SIZE, MODEL_DIMENSION), (QUERY_HEADS * HEAD_SIZE) ** -0.5, 0.078125, ((0, 8), (1, 32))),
        "cache_keys": draw_cache_keys(jax.random.fold_in(key_list[10], 71), 0),
        "earlier_values": scatter_about(key_list[7], (KEY_VALUE_HEADS, CACHE_POSITIONS, HEAD_SIZE), 1.0, 6.0, ((0, 8), (1, 32))),
        "cache_len": draw_cache_len(jax.random.fold_in(key_list[10], 71), 0),
        "stretch_start": jax.random.randint(key_list[9], (1,), 0, 4194304).astype(jnp.int32),
    }


neg_large = -1e+30

def block_stats(queries, key_block, value_block, key_mask):
    scores = jnp.einsum('rkgd,kjd->rkgj', queries.astype(jnp.float32), key_block.astype(jnp.float32))
    scores = jnp.where(key_mask, scores, neg_large)
    maximum = lax.optimization_barrier(jnp.max(scores, axis=-1))
    weights = jnp.where(key_mask, jnp.exp(scores - maximum[..., None]), 0.0)
    denominator = lax.optimization_barrier(jnp.sum(weights, axis=-1))
    rounded = lax.optimization_barrier(weights.astype(jnp.bfloat16)).astype(jnp.float32)
    numerator = jnp.einsum('rkgj,kjd->rkgd', rounded, value_block.astype(jnp.float32))
    return (maximum, denominator, numerator)

def combine(first, second):
    max_one, den_one, num_one = first
    max_two, den_two, num_two = second
    maximum = jnp.maximum(max_one, max_two)
    scale_one = jnp.exp(max_one - maximum)
    scale_two = jnp.exp(max_two - maximum)
    return (maximum, den_one * scale_one + den_two * scale_two, num_one * scale_one[..., None] + num_two * scale_two[..., None])

def reference(hidden, norm_gain, w_query, key_projection_weight, value_projection_weight, w_out, cache_keys, earlier_values, cache_len, stretch_start):
    query_group_count = QUERY_HEADS // KEY_VALUE_HEADS
    stream = hidden.astype(jnp.float32)
    normed = (stream * lax.rsqrt(lax.optimization_barrier(jnp.mean(stream * stream, axis=-1, keepdims=True)) + 1e-05) * norm_gain).astype(jnp.bfloat16)
    queries = jnp.dot(normed, w_query, preferred_element_type=jnp.float32).astype(jnp.bfloat16)
    fresh_keys = jnp.dot(normed, key_projection_weight, preferred_element_type=jnp.float32).astype(jnp.bfloat16)
    fresh_values = jnp.dot(normed, value_projection_weight, preferred_element_type=jnp.float32).astype(jnp.bfloat16)
    positions = stretch_start[0] + jnp.arange(STRETCH_TOKENS, dtype=jnp.int32)
    temper = jnp.log(((positions + 1) // 8192).astype(jnp.float32) + 1.0) * 0.1 + 1.0
    scaled_scores = (lax.optimization_barrier(queries).astype(jnp.float32) * (temper * HEAD_SIZE ** (-0.5))[:, None]).astype(jnp.bfloat16)
    scaled_scores = lax.optimization_barrier(scaled_scores).reshape(STRETCH_TOKENS, KEY_VALUE_HEADS, query_group_count, HEAD_SIZE)
    span_keys = fresh_keys.reshape(STRETCH_TOKENS, KEY_VALUE_HEADS, HEAD_SIZE).transpose(1, 0, 2)
    span_values = fresh_values.reshape(STRETCH_TOKENS, KEY_VALUE_HEADS, HEAD_SIZE).transpose(1, 0, 2)
    token_order = jnp.arange(STRETCH_TOKENS, dtype=jnp.int32)
    causal = (token_order[None, :] <= token_order[:, None])[:, None, None, :]
    running = block_stats(scaled_scores, span_keys, span_values, causal)

    def visit(carried, shard_index):
        first_key = shard_index * CACHE_DEV
        key_block = lax.dynamic_slice_in_dim(cache_keys, first_key, CACHE_DEV, 1)
        value_block = lax.dynamic_slice_in_dim(earlier_values, first_key, CACHE_DEV, 1)
        key_mask = (jnp.arange(CACHE_DEV, dtype=jnp.int32) < cache_len[shard_index])[None, None, None, :]
        return (combine(carried, block_stats(scaled_scores, key_block, value_block, key_mask)), None)
    running, _ = lax.scan(visit, running, jnp.arange(N_BLK, dtype=jnp.int32))
    maximum, denominator, numerator = running
    context = (numerator / denominator[..., None]).astype(jnp.bfloat16).reshape(STRETCH_TOKENS, QUERY_HEADS * HEAD_SIZE)
    return jnp.dot(context, w_out, preferred_element_type=jnp.float32).astype(jnp.bfloat16)
```

```python
import functools

import jax
import jax.numpy as jnp
from jax import lax
from jax.experimental import pallas as pl
from jax.experimental.pallas import tpu as pltpu
from jax.sharding import Mesh
from jax.sharding import PartitionSpec as P

BLK = ("z", "y", "c")
BF = jnp.bfloat16
F32 = jnp.float32
NEG = -1e30
KEYS = 512


def shift(x, axis, d):
    n = lax.axis_size(axis)
    return lax.ppermute(x, axis, [(i, (i + d) % n) for i in range(n)])


def ring(x, axis):
    n = lax.axis_size(axis)
    ahead, behind = [x], [x]
    for step in range(n // 2):
        ahead.append(shift(ahead[-1], axis, 1))
        if step < (n - 1) // 2:
            behind.append(shift(behind[-1], axis, -1))
    return ahead + behind[:0:-1]


def nt(a, b):
    return lax.dot_general(a, b, (((1,), (1,)), ((), ())), preferred_element_type=F32)


def tn(a, b):
    return lax.dot_general(a, b, (((0,), (0,)), ((), ())), preferred_element_type=F32)


VM = pl.BlockSpec(memory_space=pltpu.VMEM)
SM = pl.BlockSpec(memory_space=pltpu.SMEM)


def params(mib=56):
    return pltpu.CompilerParams(vmem_limit_bytes=mib << 20)


def project(where, x, blocks):
    rows, _ = x.shape
    n = len(blocks)
    r, cols = blocks[0].shape
    t = rows // 4

    def kernel(where_ref, x_ref, *refs):
        w_refs, (keep, send, whole, total) = refs[:n], refs[n:]
        z, c = where_ref[0], where_ref[2]
        for d in range(n):
            at = lax.rem(z + (n - d), n)
            whole[pl.ds(pl.multiple_of(at * r, 16), r), :] = w_refs[d][...]
        total[...] = jnp.dot(x_ref[...], whole[...], preferred_element_type=F32).reshape(4, t, cols)
        for y in range(2):
            keep[y] = total[2 * y + c]
            send[y] = total[2 * y + 1 - c]

    half = jax.ShapeDtypeStruct((2, t, cols), F32)
    return pl.pallas_call(
        kernel,
        out_shape=[half, half],
        in_specs=[SM, VM] + [VM] * n,
        out_specs=[VM, VM],
        scratch_shapes=[pltpu.VMEM((n * r, cols), BF), pltpu.VMEM((4, t, cols), F32)],
        compiler_params=params(),
        name="project",
    )(where, x, *blocks)


def pack_cache(lens, keys, values):
    n = len(keys)
    rows, d = keys[0].shape
    room = n * rows + 4 * KEYS

    def kernel(len_ref, *refs):
        k_in, v_in, (k_out, v_out) = refs[:n], refs[n : 2 * n], refs[2 * n :]
        first = k_in[0][0:1, :]
        at = jnp.int32(0)
        for i in range(n):
            length = len_ref[i]
            at = pl.multiple_of(at, 16)
            k_out[pl.ds(at, rows), :] = k_in[i][...]
            v_out[pl.ds(at, rows), :] = v_in[i][...]
            whole = length // 16
            odd = length - whole * 16
            tail = pl.multiple_of(at + whole * 16, 16)

            @pl.when(odd > 0)
            def _():
                counted = lax.broadcasted_iota(jnp.int32, (16, d), 0) < odd
                k_tile = k_out[pl.ds(tail, 16), :].astype(F32)
                v_tile = v_out[pl.ds(tail, 16), :].astype(F32)
                k_out[pl.ds(tail, 16), :] = jnp.where(counted, k_tile, first.astype(F32)).astype(BF)
                v_out[pl.ds(tail, 16), :] = jnp.where(counted, v_tile, 0.0).astype(BF)

            at = at + ((length + 15) // 16) * 16
        at = pl.multiple_of(at, 16)
        k_out[pl.ds(at, 2 * KEYS), :] = jnp.broadcast_to(first, (2 * KEYS, d))
        v_out[pl.ds(at, 2 * KEYS), :] = jnp.zeros((2 * KEYS, d), BF)

    out = jax.ShapeDtypeStruct((room, d), BF)
    return pl.pallas_call(
        kernel,
        out_shape=[out, out],
        in_specs=[SM] + [VM] * (2 * n),
        out_specs=[VM, VM],
        compiler_params=params(),
        name="pack_cache",
    )(lens, *keys, *values)


def attend(lens, where, chunks, dists, k_all, v_all, new_pairs):
    n = len(chunks)
    t, width = chunks[0].shape
    d = k_all.shape[1]
    g = width // d
    rows = n * g * t
    shards = lens.shape[0]
    fresh = new_pairs[0][0].shape[0]

    def kernel(len_ref, where_ref, *refs):
        q_refs = refs[:n]
        k_ref, v_ref, nk0, nv0, nk1, nv1 = refs[n : n + 6]
        outs = refs[n + 6 : 2 * n + 6]
        q_all, m, l, acc, s_a, s_b, token, stats = refs[2 * n + 6 :]
        z, y, c = where_ref[0], where_ref[1], where_ref[2]
        nz = where_ref[3]
        for i in range(n):
            base = lax.rem(z + nz - dists[i], nz) * (4 * t) + (2 * y + c) * t
            for h in range(g):
                at = (i * g + h) * t
                q_all[at : at + t, :] = q_refs[i][:, h * d : (h + 1) * d]
            span = slice(i * g * t, (i + 1) * g * t)
            token[:, span] = base + lax.rem(lax.broadcasted_iota(jnp.int32, (1, g * t), 1), t)
        m[...] = jnp.full(m.shape, NEG, F32)
        l[...] = jnp.zeros(l.shape, F32)
        acc[...] = jnp.zeros(acc.shape, F32)

        def scores(at):
            return nt(k_ref[pl.ds(pl.multiple_of(at, KEYS), KEYS), :], q_all[...])

        def absorb(s, values):
            before = m[...]
            now = jnp.maximum(before, jnp.max(s, axis=0, keepdims=True))
            fade = jnp.exp(before - now)
            p = jnp.exp(s - now)
            l[...] = l[...] * fade + jnp.sum(p, axis=0, keepdims=True)
            m[...] = now
            acc[...] = acc[...] * fade + tn(values, p.astype(BF))

        def values_at(at):
            return v_ref[pl.ds(pl.multiple_of(at, KEYS), KEYS), :]

        counted = jnp.int32(0)
        used = jnp.int32(0)
        for i in range(shards):
            counted = counted + len_ref[i]
            used = used + ((len_ref[i] + 15) // 16) * 16
        pairs = (used + 2 * KEYS - 1) // (2 * KEYS)
        s_a[...] = scores(0)

        def visit(u, _):
            at = u * (2 * KEYS)
            s_b[...] = scores(at + KEYS)
            absorb(s_a[...], values_at(at))
            s_a[...] = scores(at + 2 * KEYS)
            absorb(s_b[...], values_at(at + KEYS))
            return 0

        lax.fori_loop(0, pairs, visit, 0)
        extra = (pairs * (2 * KEYS) - counted).astype(F32)
        first = nt(k_ref[0:8, :], q_all[...])[0:1]
        l[...] = l[...] - extra * jnp.exp(first - m[...])
        for part, (nk, nv) in enumerate(((nk0, nv0), (nk1, nv1))):
            row = lax.broadcasted_iota(jnp.int32, (fresh, 1), 0)
            side = c if part == 0 else 1 - c
            key_token = z * (4 * t) + (row // t) * (2 * t) + side * t + lax.rem(row, t)
            s = nt(nk[...], q_all[...])
            s = jnp.where(key_token <= token[...], s, NEG)
            absorb(s, nv[...])
        top = m[...]
        top_hi = top.astype(BF).astype(F32)
        top_lo = (top - top_hi).astype(BF).astype(F32)
        scale = jnp.exp(top - (top_hi + top_lo))
        den = l[...] * scale
        den_hi = den.astype(BF).astype(F32)
        den_lo = den - den_hi
        numer = (acc[...] * scale).T
        stats[...] = jnp.zeros(stats.shape, F32)
        for i in range(n):
            for h in range(g):
                at = slice((i * g + h) * t, (i * g + h + 1) * t)
                outs[i][:, h * d : (h + 1) * d] = numer[at].astype(BF)
                for k, row in enumerate((top_hi, top_lo, den_hi, den_lo)):
                    stats[8 * k + h : 8 * k + h + 1, :] = row[:, at]
            outs[i][:, g * d :] = stats[...].T.astype(BF)

    out = jax.ShapeDtypeStruct((t, width + 128), BF)
    return pl.pallas_call(
        kernel,
        out_shape=[out] * n,
        in_specs=[SM, SM] + [VM] * (n + 6),
        out_specs=[VM] * n,
        scratch_shapes=[
            pltpu.VMEM((rows, d), BF),
            pltpu.VMEM((1, rows), F32),
            pltpu.VMEM((1, rows), F32),
            pltpu.VMEM((d, rows), F32),
            pltpu.VMEM((KEYS, rows), F32),
            pltpu.VMEM((KEYS, rows), F32),
            pltpu.VMEM((1, rows), jnp.int32),
            pltpu.VMEM((128, t), F32),
        ],
        compiler_params=params(),
        name="attend",
    )(lens, where, *chunks, k_all, v_all, *new_pairs[0], *new_pairs[1])


def merge(parts, d):
    n = len(parts)
    t, width = parts[0].shape
    g = (width - 128) // d

    def kernel(*refs):
        ins, out = refs[:n], refs[n]
        stats = [r[:, g * d :].astype(F32) for r in ins]
        for h in range(g):
            tops = [s[:, h : h + 1] + s[:, 8 + h : 9 + h] for s in stats]
            dens = [s[:, 16 + h : 17 + h] + s[:, 24 + h : 25 + h] for s in stats]
            top = functools.reduce(jnp.maximum, tops)
            shares = [jnp.exp(a - top) for a in tops]
            den = sum(w * a for w, a in zip(shares, dens))
            num = sum(w * r[:, h * d : (h + 1) * d].astype(F32) for w, r in zip(shares, ins))
            out[:, h * d : (h + 1) * d] = (num / den).astype(BF)

    return pl.pallas_call(
        kernel,
        out_shape=jax.ShapeDtypeStruct((t, g * d), BF),
        in_specs=[VM] * n,
        out_specs=VM,
        compiler_params=params(),
        name="merge",
    )(*parts)


def per_device(
    hidden,
    norm_gain,
    w_query,
    key_projection_weight,
    value_projection_weight,
    w_out,
    cache_keys,
    earlier_values,
    cache_len,
    stretch_start,
):
    t, model = hidden.shape
    d = cache_keys.shape[2]
    q_cols = w_query.shape[1]
    kv_cols = key_projection_weight.shape[1]
    nz = lax.axis_size("z")
    nh = lax.axis_size("head")
    z, y, c = lax.axis_index("z"), lax.axis_index("y"), lax.axis_index("c")
    where = jnp.stack([z, y, c, jnp.int32(nz)]).astype(jnp.int32)

    weights = jnp.concatenate([w_query, key_projection_weight, value_projection_weight], axis=1)
    blocks = ring(weights, "z")

    stream = hidden.astype(F32)
    normed = (
        stream * lax.rsqrt(jnp.mean(stream * stream, axis=-1, keepdims=True) + 1e-05) * norm_gain
    ).astype(BF)
    cut = normed.reshape(t, nz, 4, model // (4 * nz)).transpose(2, 0, 1, 3).reshape(4, t, model // 4)
    x = lax.all_to_all(cut, ("y", "c"), 0, 0, tiled=True).reshape(4 * t, model // 4)

    near = (cache_keys[0], earlier_values[0], cache_len)
    beside = tuple(shift(a, "y", 1) for a in near)
    four = [near, beside] + [tuple(shift(a, "c", 1) for a in s) for s in (near, beside)]
    lens = jnp.concatenate([s[2] for s in four])
    k_all, v_all = pack_cache(lens, [s[0] for s in four], [s[1] for s in four])

    out_beside = shift(w_out, "y", 1)
    out_four = [w_out, shift(w_out, "c", 1), out_beside, shift(out_beside, "c", 1)]

    keep, send = project(where, x, blocks)
    both = keep + shift(send, "c", 1)
    q_near = lax.dynamic_index_in_dim(both, y, 0, keepdims=False)[:, :q_cols]
    q_away = lax.dynamic_index_in_dim(both, 1 - y, 0, keepdims=False)[:, :q_cols]
    kv = both[:, :, q_cols:]
    queries = (q_near + shift(q_away, "y", 1)).astype(BF)
    fresh = (kv + shift(kv, "y", 1)).astype(BF).reshape(2 * t, 2 * kv_cols)
    other = shift(fresh, "c", 1)
    new_pairs = [(f[:, :kv_cols], f[:, kv_cols:]) for f in (fresh, other)]

    token = lax.axis_index(BLK) * t + jnp.arange(t, dtype=jnp.int32)
    positions = stretch_start[0] + token
    temper = jnp.log(((positions + 1) // 8192).astype(F32) + 1.0) * 0.1 + 1.0
    scaled = (
        lax.optimization_barrier(queries).astype(F32) * (temper * d ** (-0.5))[:, None]
    ).astype(BF)

    chunks = ring(scaled, "z")
    partial = attend(lens, where, chunks, list(range(nz)), k_all, v_all, new_pairs)
    order = lax.rem(z - jnp.arange(nz) + nz, nz)
    stacked = jnp.stack(partial)[order]
    returned = lax.all_to_all(stacked, "z", 0, 0, tiled=True)
    context = merge([returned[i] for i in range(nz)], d)

    spread = lax.all_gather(context, "z", axis=0, tiled=False)
    tokens = spread.reshape(nz * t, q_cols)
    terms = [jnp.dot(tokens, w, preferred_element_type=F32).astype(BF) for w in out_four]
    terms = jnp.stack(terms, 1).reshape(nz, t, 4, -1).transpose(0, 2, 1, 3)
    summed = lax.all_to_all(terms, "head", 0, 0, tiled=True).astype(F32).sum(axis=0).astype(BF)
    here = 2 * y + c
    summed = summed[jnp.arange(4) ^ here]
    final = lax.all_to_all(summed, ("y", "c"), 0, 0, tiled=True)
    return final.reshape(4 * t, -1)


def solution(mesh):
    finer = Mesh(mesh.devices.reshape(8, 2, 2, mesh.shape["head"]), ("z", "y", "c", "head"))
    return jax.shard_map(
        per_device,
        mesh=finer,
        in_specs=(
            P(BLK, None),
            P(),
            P(BLK, "head"),
            P(BLK, "head"),
            P(BLK, "head"),
            P("head", BLK),
            P("head", BLK, None),
            P("head", BLK, None),
            P(BLK),
            P(),
        ),
        out_specs=P("head", BLK),
        check_vma=False,
    )
```

```python
import functools

import jax
import jax.numpy as jnp
from jax import lax
from jax.experimental import pallas as pl
from jax.experimental.pallas import tpu as pltpu
from jax.sharding import Mesh
from jax.sharding import PartitionSpec as P

BLK = ("z", "y", "c")
BF = jnp.bfloat16
F32 = jnp.float32
NEG = -1e30
KEYS = 512


def shift(x, axis, d):
    n = lax.axis_size(axis)
    return lax.ppermute(x, axis, [(i, (i + d) % n) for i in range(n)])


def ring(x, axis, before_last=None):
    n = lax.axis_size(axis)
    ahead, behind = [x], [x]
    for step in range(n // 2):
        if before_last is not None and step == n // 2 - 1:
            ahead[-1], before_last = lax.optimization_barrier((ahead[-1], before_last))
        ahead.append(shift(ahead[-1], axis, 1))
        if step < (n - 1) // 2:
            behind.append(shift(behind[-1], axis, -1))
    blocks = ahead + behind[:0:-1]
    return blocks if before_last is None else (blocks, before_last)


def nt(a, b):
    return lax.dot_general(a, b, (((1,), (1,)), ((), ())), preferred_element_type=F32)


def tn(a, b):
    return lax.dot_general(a, b, (((0,), (0,)), ((), ())), preferred_element_type=F32)


VM = pl.BlockSpec(memory_space=pltpu.VMEM)
SM = pl.BlockSpec(memory_space=pltpu.SMEM)


def params(mib=56):
    return pltpu.CompilerParams(vmem_limit_bytes=mib << 20)


def side_by_side(arrays):
    rows = arrays[0].shape[0]
    widths = [a.shape[1] for a in arrays]

    def body(*refs):
        out, at = refs[-1], 0
        for ref, width in zip(refs[:-1], widths):
            out[:, at : at + width] = ref[...]
            at += width

    return pl.pallas_call(
        body,
        out_shape=jax.ShapeDtypeStruct((rows, sum(widths)), arrays[0].dtype),
        in_specs=[VM] * len(arrays),
        out_specs=VM,
        compiler_params=params(),
        name="side_by_side",
    )(*arrays)


def project(where, x, blocks):
    rows, _ = x.shape
    n = len(blocks)
    r, cols = blocks[0].shape
    t = rows // 4

    def kernel(where_ref, x_ref, *refs):
        w_refs, (keep, send, whole, total) = refs[:n], refs[n:]
        z, c = where_ref[0], where_ref[2]
        for d in range(n):
            at = lax.rem(z + (n - d), n)
            whole[pl.ds(pl.multiple_of(at * r, 16), r), :] = w_refs[d][...]
        total[...] = jnp.dot(x_ref[...], whole[...], preferred_element_type=F32).reshape(4, t, cols)
        for y in range(2):
            keep[y] = total[2 * y + c]
            send[y] = total[2 * y + 1 - c]

    half = jax.ShapeDtypeStruct((2, t, cols), F32)
    return pl.pallas_call(
        kernel,
        out_shape=[half, half],
        in_specs=[SM, VM] + [VM] * n,
        out_specs=[VM, VM],
        scratch_shapes=[pltpu.VMEM((n * r, cols), BF), pltpu.VMEM((4, t, cols), F32)],
        compiler_params=params(),
        name="project",
    )(where, x, *blocks)


def pack_cache(lens, keys, values):
    n = len(keys)
    rows, d = keys[0].shape
    room = n * rows + 4 * KEYS

    def kernel(len_ref, *refs):
        k_in, v_in, (k_out, v_out) = refs[:n], refs[n : 2 * n], refs[2 * n :]
        first = k_in[0][0:1, :]
        at = jnp.int32(0)
        for i in range(n):
            length = len_ref[i]
            at = pl.multiple_of(at, 16)
            k_out[pl.ds(at, rows), :] = k_in[i][...]
            v_out[pl.ds(at, rows), :] = v_in[i][...]
            whole = length // 16
            odd = length - whole * 16
            tail = pl.multiple_of(at + whole * 16, 16)

            @pl.when(odd > 0)
            def _():
                counted = lax.broadcasted_iota(jnp.int32, (16, d), 0) < odd
                k_tile = k_out[pl.ds(tail, 16), :].astype(F32)
                v_tile = v_out[pl.ds(tail, 16), :].astype(F32)
                k_out[pl.ds(tail, 16), :] = jnp.where(counted, k_tile, first.astype(F32)).astype(BF)
                v_out[pl.ds(tail, 16), :] = jnp.where(counted, v_tile, 0.0).astype(BF)

            at = at + ((length + 15) // 16) * 16
        at = pl.multiple_of(at, 16)
        k_out[pl.ds(at, 2 * KEYS), :] = jnp.broadcast_to(first, (2 * KEYS, d))
        v_out[pl.ds(at, 2 * KEYS), :] = jnp.zeros((2 * KEYS, d), BF)

    out = jax.ShapeDtypeStruct((room, d), BF)
    return pl.pallas_call(
        kernel,
        out_shape=[out, out],
        in_specs=[SM] + [VM] * (2 * n),
        out_specs=[VM, VM],
        compiler_params=params(),
        name="pack_cache",
    )(lens, *keys, *values)


def attend(lens, where, chunks, dists, k_all, v_all, new_pairs):
    n = len(chunks)
    t, width = chunks[0].shape
    d = k_all.shape[1]
    g = width // d
    rows = n * g * t
    shards = lens.shape[0]
    fresh = new_pairs[0][0].shape[0]

    def kernel(len_ref, where_ref, *refs):
        q_refs = refs[:n]
        k_ref, v_ref, nk0, nv0, nk1, nv1 = refs[n : n + 6]
        out = refs[n + 6]
        q_all, m, l, acc, s_a, s_b, token, stats = refs[n + 7 :]
        z, y, c = where_ref[0], where_ref[1], where_ref[2]
        nz = where_ref[3]
        for i in range(n):
            base = lax.rem(z + nz - dists[i], nz) * (4 * t) + (2 * y + c) * t
            for h in range(g):
                at = (i * g + h) * t
                q_all[at : at + t, :] = q_refs[i][:, h * d : (h + 1) * d]
            span = slice(i * g * t, (i + 1) * g * t)
            token[:, span] = base + lax.rem(lax.broadcasted_iota(jnp.int32, (1, g * t), 1), t)
        m[...] = jnp.full(m.shape, NEG, F32)
        l[...] = jnp.zeros(l.shape, F32)
        acc[...] = jnp.zeros(acc.shape, F32)

        def scores(at):
            return nt(k_ref[pl.ds(pl.multiple_of(at, KEYS), KEYS), :], q_all[...])

        def absorb(s, values):
            before = m[...]
            now = jnp.maximum(before, jnp.max(s, axis=0, keepdims=True))
            fade = jnp.exp(before - now)
            p = jnp.exp(s - now)
            l[...] = l[...] * fade + jnp.sum(p, axis=0, keepdims=True)
            m[...] = now
            acc[...] = acc[...] * fade + tn(values, p.astype(BF))

        def values_at(at):
            return v_ref[pl.ds(pl.multiple_of(at, KEYS), KEYS), :]

        counted = jnp.int32(0)
        used = jnp.int32(0)
        for i in range(shards):
            counted = counted + len_ref[i]
            used = used + ((len_ref[i] + 15) // 16) * 16
        pairs = (used + 2 * KEYS - 1) // (2 * KEYS)
        s_a[...] = scores(0)

        def visit(u, _):
            at = u * (2 * KEYS)
            s_b[...] = scores(at + KEYS)
            absorb(s_a[...], values_at(at))
            s_a[...] = scores(at + 2 * KEYS)
            absorb(s_b[...], values_at(at + KEYS))
            return 0

        lax.fori_loop(0, pairs, visit, 0)
        extra = (pairs * (2 * KEYS) - counted).astype(F32)
        first = nt(k_ref[0:8, :], q_all[...])[0:1]
        l[...] = l[...] - extra * jnp.exp(first - m[...])
        for part, (nk, nv) in enumerate(((nk0, nv0), (nk1, nv1))):
            row = lax.broadcasted_iota(jnp.int32, (fresh, 1), 0)
            side = c if part == 0 else 1 - c
            key_token = z * (4 * t) + (row // t) * (2 * t) + side * t + lax.rem(row, t)
            s = nt(nk[...], q_all[...])
            s = jnp.where(key_token <= token[...], s, NEG)
            absorb(s, nv[...])
        top = m[...]
        top_hi = top.astype(BF).astype(F32)
        top_lo = (top - top_hi).astype(BF).astype(F32)
        scale = jnp.exp(top - (top_hi + top_lo))
        den = l[...] * scale
        den_hi = den.astype(BF).astype(F32)
        den_lo = den - den_hi
        numer = (acc[...] * scale).T
        stats[...] = jnp.zeros(stats.shape, F32)
        for i in range(n):
            owner = lax.rem(z + nz - dists[i], nz)
            for h in range(g):
                at = slice((i * g + h) * t, (i * g + h + 1) * t)
                out[owner, :, h * d : (h + 1) * d] = numer[at].astype(BF)
                for k, row in enumerate((top_hi, top_lo, den_hi, den_lo)):
                    stats[8 * k + h : 8 * k + h + 1, :] = row[:, at]
            out[owner, :, g * d :] = stats[...].T.astype(BF)

    return pl.pallas_call(
        kernel,
        out_shape=jax.ShapeDtypeStruct((n, t, width + 128), BF),
        in_specs=[SM, SM] + [VM] * (n + 6),
        out_specs=VM,
        scratch_shapes=[
            pltpu.VMEM((rows, d), BF),
            pltpu.VMEM((1, rows), F32),
            pltpu.VMEM((1, rows), F32),
            pltpu.VMEM((d, rows), F32),
            pltpu.VMEM((KEYS, rows), F32),
            pltpu.VMEM((KEYS, rows), F32),
            pltpu.VMEM((1, rows), jnp.int32),
            pltpu.VMEM((128, t), F32),
        ],
        compiler_params=params(),
        name="attend",
    )(lens, where, *chunks, k_all, v_all, *new_pairs[0], *new_pairs[1])


def merge(parts, d):
    n, t, width = parts.shape
    g = (width - 128) // d

    def kernel(ins, out):
        stats = [ins[i, :, g * d :].astype(F32) for i in range(n)]
        for h in range(g):
            tops = [s[:, h : h + 1] + s[:, 8 + h : 9 + h] for s in stats]
            dens = [s[:, 16 + h : 17 + h] + s[:, 24 + h : 25 + h] for s in stats]
            top = functools.reduce(jnp.maximum, tops)
            shares = [jnp.exp(a - top) for a in tops]
            den = sum(w * a for w, a in zip(shares, dens))
            num = sum(w * ins[i, :, h * d : (h + 1) * d].astype(F32) for i, w in enumerate(shares))
            out[:, h * d : (h + 1) * d] = (num / den).astype(BF)

    return pl.pallas_call(
        kernel,
        out_shape=jax.ShapeDtypeStruct((t, g * d), BF),
        in_specs=[VM],
        out_specs=VM,
        compiler_params=params(),
        name="merge",
    )(parts)


def project_out(where, contexts, weights):
    n = len(contexts)
    t, inner = contexts[0].shape
    cols = weights[0].shape[0]

    def kernel(where_ref, *refs):
        c_refs, w_refs = refs[:n], refs[n : n + 4]
        out, tokens, w_all = refs[n + 4 :]
        z, here = where_ref[0], 2 * where_ref[1] + where_ref[2]
        for i in range(n):
            tokens[lax.rem(z + (n - i), n)] = c_refs[i][...]
        for f in range(4):
            w_all[f ^ here] = w_refs[f][...]
        res = nt(tokens[...].reshape(n * t, inner), w_all[...].reshape(4 * cols, inner))
        out[...] = res.astype(BF).reshape(n, t, 4 * cols)

    return pl.pallas_call(
        kernel,
        out_shape=jax.ShapeDtypeStruct((n, t, 4 * cols), BF),
        in_specs=[SM] + [VM] * (n + 4),
        out_specs=VM,
        scratch_shapes=[
            pltpu.VMEM((n, t, inner), BF),
            pltpu.VMEM((4, cols, inner), BF),
        ],
        compiler_params=params(),
        name="project_out",
    )(where, *contexts, *weights)


def per_device(
    hidden,
    norm_gain,
    w_query,
    key_projection_weight,
    value_projection_weight,
    w_out,
    cache_keys,
    earlier_values,
    cache_len,
    stretch_start,
):
    t, model = hidden.shape
    d = cache_keys.shape[2]
    q_cols = w_query.shape[1]
    kv_cols = key_projection_weight.shape[1]
    nz = lax.axis_size("z")
    z, y, c = lax.axis_index("z"), lax.axis_index("y"), lax.axis_index("c")
    where = jnp.stack([z, y, c, jnp.int32(nz)]).astype(jnp.int32)

    near = (cache_keys[0], earlier_values[0], cache_len)
    beside = tuple(shift(a, "y", 1) for a in near)
    weights = side_by_side([w_query, key_projection_weight, value_projection_weight])
    blocks, beside = ring(weights, "z", beside)

    stream = hidden.astype(F32)
    normed = (
        stream * lax.rsqrt(jnp.mean(stream * stream, axis=-1, keepdims=True) + 1e-05) * norm_gain
    ).astype(BF)
    cut = normed.reshape(t, nz, 4, model // (4 * nz)).transpose(2, 0, 1, 3).reshape(4, t, model // 4)
    x = lax.all_to_all(cut, ("y", "c"), 0, 0, tiled=True).reshape(4 * t, model // 4)

    four = [near, beside] + [tuple(shift(a, "c", 1) for a in s) for s in (near, beside)]
    lens = jnp.concatenate([s[2] for s in four])
    k_all, v_all = pack_cache(lens, [s[0] for s in four], [s[1] for s in four])
    x, k_all, v_all = lax.optimization_barrier((x, k_all, v_all))

    out_near = w_out.T
    out_beside = shift(out_near, "y", 1)
    out_four = [out_near, shift(out_near, "c", 1), out_beside, shift(out_beside, "c", 1)]

    keep, send = project(where, x, blocks)
    both = keep + shift(send, "c", 1)
    q_near = lax.dynamic_index_in_dim(both, y, 0, keepdims=False)[:, :q_cols]
    q_away = lax.dynamic_index_in_dim(both, 1 - y, 0, keepdims=False)[:, :q_cols]
    kv = both[:, :, q_cols:]
    queries = (q_near + shift(q_away, "y", 1)).astype(BF)
    fresh = (kv + shift(kv, "y", 1)).astype(BF).reshape(2 * t, 2 * kv_cols)
    other = shift(fresh, "c", 1)
    new_pairs = [(f[:, :kv_cols], f[:, kv_cols:]) for f in (fresh, other)]

    token = lax.axis_index(BLK) * t + jnp.arange(t, dtype=jnp.int32)
    positions = stretch_start[0] + token
    temper = jnp.log(((positions + 1) // 8192).astype(F32) + 1.0) * 0.1 + 1.0
    scaled = (
        lax.optimization_barrier(queries).astype(F32) * (temper * d ** (-0.5))[:, None]
    ).astype(BF)

    chunks = ring(scaled, "z")
    partial = attend(lens, where, chunks, list(range(nz)), k_all, v_all, new_pairs)
    returned = lax.all_to_all(partial, "z", 0, 0, tiled=True)
    context = merge(returned, d)

    terms = project_out(where, ring(context, "z"), out_four)
    summed = lax.all_to_all(terms, "head", 0, 0, tiled=True).astype(F32).sum(axis=0).astype(BF)
    final = lax.all_to_all(summed.reshape(t, 4, -1).transpose(1, 0, 2), ("y", "c"), 0, 0, tiled=True)
    return final.reshape(4 * t, -1)


def solution(mesh):
    finer = Mesh(mesh.devices.reshape(8, 2, 2, mesh.shape["head"]), ("z", "y", "c", "head"))
    return jax.shard_map(
        per_device,
        mesh=finer,
        in_specs=(
            P(BLK, None),
            P(),
            P(BLK, "head"),
            P(BLK, "head"),
            P(BLK, "head"),
            P("head", BLK),
            P("head", BLK, None),
            P("head", BLK, None),
            P(BLK),
            P(),
        ),
        out_specs=P("head", BLK),
        check_vma=False,
    )
```

```python
import functools

import jax
import jax.numpy as jnp
from jax import lax
from jax.experimental import pallas as pl
from jax.experimental.pallas import tpu as pltpu
from jax.sharding import Mesh
from jax.sharding import PartitionSpec as P

BLK = ("z", "y", "c")
BF = jnp.bfloat16
F32 = jnp.float32
NEG = -1e30
KEYS = 512


def shift(x, axis, d):
    n = lax.axis_size(axis)
    return lax.ppermute(x, axis, [(i, (i + d) % n) for i in range(n)])


def ring(x, axis, beside=None):
    n = lax.axis_size(axis)
    ahead, behind = [x], [x]
    for step in range(n // 2):
        if beside and step in beside:
            ahead[-1], beside[step] = lax.optimization_barrier((ahead[-1], beside[step]))
        ahead.append(shift(ahead[-1], axis, 1))
        if step < (n - 1) // 2:
            behind.append(shift(behind[-1], axis, -1))
    return ahead + behind[:0:-1]


def nt(a, b):
    return lax.dot_general(a, b, (((1,), (1,)), ((), ())), preferred_element_type=F32)


def tn(a, b):
    return lax.dot_general(a, b, (((0,), (0,)), ((), ())), preferred_element_type=F32)


VM = pl.BlockSpec(memory_space=pltpu.VMEM)
SM = pl.BlockSpec(memory_space=pltpu.SMEM)


def params(mib=56):
    return pltpu.CompilerParams(vmem_limit_bytes=mib << 20)


def side_by_side(arrays):
    rows = arrays[0].shape[0]
    widths = [a.shape[1] for a in arrays]

    def body(*refs):
        out, at = refs[-1], 0
        for ref, width in zip(refs[:-1], widths):
            out[:, at : at + width] = ref[...]
            at += width

    return pl.pallas_call(
        body,
        out_shape=jax.ShapeDtypeStruct((rows, sum(widths)), arrays[0].dtype),
        in_specs=[VM] * len(arrays),
        out_specs=VM,
        compiler_params=params(),
        name="side_by_side",
    )(*arrays)


def project(where, x, blocks):
    rows, _ = x.shape
    n = len(blocks)
    r, cols = blocks[0].shape
    t = rows // 4

    def kernel(where_ref, x_ref, *refs):
        w_refs, (keep, send, whole, total) = refs[:n], refs[n:]
        z, c = where_ref[0], where_ref[2]
        for d in range(n):
            at = lax.rem(z + (n - d), n)
            whole[pl.ds(pl.multiple_of(at * r, 16), r), :] = w_refs[d][...]
        total[...] = jnp.dot(x_ref[...], whole[...], preferred_element_type=F32).reshape(4, t, cols)
        for y in range(2):
            keep[y] = total[2 * y + c]
            send[y] = total[2 * y + 1 - c]

    half = jax.ShapeDtypeStruct((2, t, cols), F32)
    return pl.pallas_call(
        kernel,
        out_shape=[half, half],
        in_specs=[SM, VM] + [VM] * n,
        out_specs=[VM, VM],
        scratch_shapes=[pltpu.VMEM((n * r, cols), BF), pltpu.VMEM((4, t, cols), F32)],
        compiler_params=params(),
        name="project",
    )(where, x, *blocks)


def norm_cut(hidden, gain, n):
    t, model = hidden.shape
    width = model // (4 * n)

    def kernel(h_ref, g_ref, out):
        x = h_ref[...].astype(F32)
        normed = (
            x * lax.rsqrt(jnp.mean(x * x, axis=-1, keepdims=True) + 1e-05) * g_ref[...]
        ).astype(BF)
        for k in range(n):
            for j in range(4):
                at = (4 * k + j) * width
                out[j, :, k * width : (k + 1) * width] = normed[:, at : at + width]

    return pl.pallas_call(
        kernel,
        out_shape=jax.ShapeDtypeStruct((4, t, n * width), BF),
        in_specs=[VM, VM],
        out_specs=VM,
        compiler_params=params(),
        name="norm_cut",
    )(hidden, gain.reshape(1, model))


TAIL = 16


def join_cache(keys, values, length):
    rows, d = keys.shape

    def kernel(len_ref, k_ref, v_ref, out, digits, sems):
        copies = [
            pltpu.make_async_copy(k_ref, out.at[0:rows], sems.at[0]),
            pltpu.make_async_copy(v_ref, out.at[rows : 2 * rows], sems.at[1]),
            pltpu.make_async_copy(digits, out.at[2 * rows : 2 * rows + TAIL], sems.at[2]),
        ]
        copies[0].start()
        copies[1].start()
        lane = lax.broadcasted_iota(jnp.int32, (TAIL, d), 1)
        digits[...] = jnp.where(lane == 0, len_ref[0] // 64, lax.rem(len_ref[0], 64)).astype(F32).astype(BF)
        copies[2].start()
        for copy in copies:
            copy.wait()

    hbm = pl.BlockSpec(memory_space=pl.ANY)
    return pl.pallas_call(
        kernel,
        out_shape=jax.ShapeDtypeStruct((2 * rows + TAIL, d), keys.dtype),
        in_specs=[SM, hbm, hbm],
        out_specs=hbm,
        scratch_shapes=[pltpu.VMEM((TAIL, d), BF), pltpu.SemaphoreType.DMA((3,))],
        compiler_params=params(),
        name="join_cache",
    )(length, keys, values)


def joined_length(joined):
    digits = joined[-TAIL, 0:2].astype(jnp.int32)
    return digits[0:1] * 64 + digits[1:2]


def attend(lens, where, chunks, dists, caches, new_pairs):
    n = len(chunks)
    t, width = chunks[0].shape
    d = caches[0].shape[1]
    each = (caches[0].shape[0] - TAIL) // 2
    ns = len(caches)
    room = ns * each + 4 * KEYS
    g = width // d
    rows = n * g * t
    fresh = new_pairs[0][0].shape[0]

    def kernel(len_ref, where_ref, *refs):
        q_refs = refs[:n]
        c_refs = refs[n : n + ns]
        nk0, nv0, nk1, nv1 = refs[n + ns : n + ns + 4]
        out = refs[n + ns + 4]
        q_all, m, l, acc, s_a, s_b, token, stats, k_ref, v_ref = refs[n + ns + 5 :]
        top_key = c_refs[0][0:1, :]
        at = jnp.int32(0)
        for i in range(ns):
            length = len_ref[i]
            at = pl.multiple_of(at, 16)
            k_ref[pl.ds(at, each), :] = c_refs[i][0:each, :]
            v_ref[pl.ds(at, each), :] = c_refs[i][each : 2 * each, :]
            whole = length // 16
            odd = length - whole * 16
            tail = pl.multiple_of(at + whole * 16, 16)

            @pl.when(odd > 0)
            def _():
                valid = lax.broadcasted_iota(jnp.int32, (16, d), 0) < odd
                k_tile = k_ref[pl.ds(tail, 16), :].astype(F32)
                v_tile = v_ref[pl.ds(tail, 16), :].astype(F32)
                k_ref[pl.ds(tail, 16), :] = jnp.where(valid, k_tile, top_key.astype(F32)).astype(BF)
                v_ref[pl.ds(tail, 16), :] = jnp.where(valid, v_tile, 0.0).astype(BF)

            at = at + ((length + 15) // 16) * 16
        at = pl.multiple_of(at, 16)
        k_ref[pl.ds(at, 2 * KEYS), :] = jnp.broadcast_to(top_key, (2 * KEYS, d))
        v_ref[pl.ds(at, 2 * KEYS), :] = jnp.zeros((2 * KEYS, d), BF)
        z, y, c = where_ref[0], where_ref[1], where_ref[2]
        nz = where_ref[3]
        for i in range(n):
            base = lax.rem(z + nz - dists[i], nz) * (4 * t) + (2 * y + c) * t
            for h in range(g):
                at = (i * g + h) * t
                q_all[at : at + t, :] = q_refs[i][:, h * d : (h + 1) * d]
            span = slice(i * g * t, (i + 1) * g * t)
            token[:, span] = base + lax.rem(lax.broadcasted_iota(jnp.int32, (1, g * t), 1), t)
        m[...] = jnp.full(m.shape, NEG, F32)
        l[...] = jnp.zeros(l.shape, F32)
        acc[...] = jnp.zeros(acc.shape, F32)

        def scores(at):
            return nt(k_ref[pl.ds(pl.multiple_of(at, KEYS), KEYS), :], q_all[...])

        def absorb(s, values):
            before = m[...]
            now = jnp.maximum(before, jnp.max(s, axis=0, keepdims=True))
            fade = jnp.exp(before - now)
            p = jnp.exp(s - now)
            l[...] = l[...] * fade + jnp.sum(p, axis=0, keepdims=True)
            m[...] = now
            acc[...] = acc[...] * fade + tn(values, p.astype(BF))

        def values_at(at):
            return v_ref[pl.ds(pl.multiple_of(at, KEYS), KEYS), :]

        counted = jnp.int32(0)
        used = jnp.int32(0)
        for i in range(ns):
            counted = counted + len_ref[i]
            used = used + ((len_ref[i] + 15) // 16) * 16
        pairs = (used + 2 * KEYS - 1) // (2 * KEYS)
        s_a[...] = scores(0)

        def visit(u, _):
            at = u * (2 * KEYS)
            s_b[...] = scores(at + KEYS)
            absorb(s_a[...], values_at(at))
            s_a[...] = scores(at + 2 * KEYS)
            absorb(s_b[...], values_at(at + KEYS))
            return 0

        lax.fori_loop(0, pairs, visit, 0)
        extra = (pairs * (2 * KEYS) - counted).astype(F32)
        first = nt(k_ref[0:8, :], q_all[...])[0:1]
        l[...] = l[...] - extra * jnp.exp(first - m[...])
        for part, (nk, nv) in enumerate(((nk0, nv0), (nk1, nv1))):
            row = lax.broadcasted_iota(jnp.int32, (fresh, 1), 0)
            side = c if part == 0 else 1 - c
            key_token = z * (4 * t) + (row // t) * (2 * t) + side * t + lax.rem(row, t)
            s = nt(nk[...], q_all[...])
            s = jnp.where(key_token <= token[...], s, NEG)
            absorb(s, nv[...])
        top = m[...]
        top_hi = top.astype(BF).astype(F32)
        top_lo = (top - top_hi).astype(BF).astype(F32)
        scale = jnp.exp(top - (top_hi + top_lo))
        den = l[...] * scale
        den_hi = den.astype(BF).astype(F32)
        den_lo = den - den_hi
        numer = (acc[...] * scale).T
        stats[...] = jnp.zeros(stats.shape, F32)
        for i in range(n):
            owner = lax.rem(z + nz - dists[i], nz)
            for h in range(g):
                at = slice((i * g + h) * t, (i * g + h + 1) * t)
                out[owner, :, h * d : (h + 1) * d] = numer[at].astype(BF)
                for k, row in enumerate((top_hi, top_lo, den_hi, den_lo)):
                    stats[8 * k + h : 8 * k + h + 1, :] = row[:, at]
            out[owner, :, g * d :] = stats[...].T.astype(BF)

    return pl.pallas_call(
        kernel,
        out_shape=jax.ShapeDtypeStruct((n, t, width + 128), BF),
        in_specs=[SM, SM] + [VM] * (n + ns + 4),
        out_specs=VM,
        scratch_shapes=[
            pltpu.VMEM((rows, d), BF),
            pltpu.VMEM((1, rows), F32),
            pltpu.VMEM((1, rows), F32),
            pltpu.VMEM((d, rows), F32),
            pltpu.VMEM((KEYS, rows), F32),
            pltpu.VMEM((KEYS, rows), F32),
            pltpu.VMEM((1, rows), jnp.int32),
            pltpu.VMEM((128, t), F32),
            pltpu.VMEM((room, d), BF),
            pltpu.VMEM((room, d), BF),
        ],
        compiler_params=params(),
        name="attend",
    )(lens, where, *chunks, *caches, *new_pairs[0], *new_pairs[1])


def merge(parts, d):
    n, t, width = parts.shape
    g = (width - 128) // d

    def kernel(ins, out):
        stats = [ins[i, :, g * d :].astype(F32) for i in range(n)]
        for h in range(g):
            tops = [s[:, h : h + 1] + s[:, 8 + h : 9 + h] for s in stats]
            dens = [s[:, 16 + h : 17 + h] + s[:, 24 + h : 25 + h] for s in stats]
            top = functools.reduce(jnp.maximum, tops)
            shares = [jnp.exp(a - top) for a in tops]
            den = sum(w * a for w, a in zip(shares, dens))
            num = sum(w * ins[i, :, h * d : (h + 1) * d].astype(F32) for i, w in enumerate(shares))
            out[:, h * d : (h + 1) * d] = (num / den).astype(BF)

    return pl.pallas_call(
        kernel,
        out_shape=jax.ShapeDtypeStruct((t, g * d), BF),
        in_specs=[VM],
        out_specs=VM,
        compiler_params=params(),
        name="merge",
    )(parts)


def project_out(where, contexts, weights):
    n = len(contexts)
    t, inner = contexts[0].shape
    cols = weights[0].shape[0]

    def kernel(where_ref, *refs):
        c_refs, w_refs = refs[:n], refs[n : n + 4]
        out, tokens, w_all = refs[n + 4 :]
        z, here = where_ref[0], 2 * where_ref[1] + where_ref[2]
        for i in range(n):
            tokens[lax.rem(z + (n - i), n)] = c_refs[i][...]
        for f in range(4):
            w_all[f ^ here] = w_refs[f][...]
        res = nt(tokens[...].reshape(n * t, inner), w_all[...].reshape(4 * cols, inner))
        out[...] = res.astype(BF).reshape(n, t, 4 * cols)

    return pl.pallas_call(
        kernel,
        out_shape=jax.ShapeDtypeStruct((n, t, 4 * cols), BF),
        in_specs=[SM] + [VM] * (n + 4),
        out_specs=VM,
        scratch_shapes=[
            pltpu.VMEM((n, t, inner), BF),
            pltpu.VMEM((4, cols, inner), BF),
        ],
        compiler_params=params(),
        name="project_out",
    )(where, *contexts, *weights)


def per_device(
    hidden,
    norm_gain,
    w_query,
    key_projection_weight,
    value_projection_weight,
    w_out,
    cache_keys,
    earlier_values,
    cache_len,
    stretch_start,
):
    t, model = hidden.shape
    d = cache_keys.shape[2]
    q_cols = w_query.shape[1]
    kv_cols = key_projection_weight.shape[1]
    nz = lax.axis_size("z")
    z, y, c = lax.axis_index("z"), lax.axis_index("y"), lax.axis_index("c")
    where = jnp.stack([z, y, c, jnp.int32(nz)]).astype(jnp.int32)

    cut = norm_cut(hidden, norm_gain, nz)
    x = lax.all_to_all(cut, ("y", "c"), 0, 0, tiled=True).reshape(4 * t, model // 4)
    near = join_cache(cache_keys[0], earlier_values[0], cache_len)

    weights = side_by_side([w_query, key_projection_weight, value_projection_weight])
    beside = {1: near, 2: x}
    blocks = ring(weights, "z", beside)
    near, x = beside[1], beside[2]

    beside = shift(near, "y", 1)
    caches = [near, beside, shift(near, "c", 1), shift(beside, "c", 1)]
    lens = jnp.concatenate([joined_length(a) for a in caches])

    keep, send = project(where, x, blocks)
    both = keep + shift(send, "c", 1)
    q_near = lax.dynamic_index_in_dim(both, y, 0, keepdims=False)[:, :q_cols]
    q_away = lax.dynamic_index_in_dim(both, 1 - y, 0, keepdims=False)[:, :q_cols]
    kv = both[:, :, q_cols:]
    queries = (q_near + shift(q_away, "y", 1)).astype(BF)
    fresh = (kv + shift(kv, "y", 1)).astype(BF).reshape(2 * t, 2 * kv_cols)
    other = shift(fresh, "c", 1)
    new_pairs = [(f[:, :kv_cols], f[:, kv_cols:]) for f in (fresh, other)]

    token = lax.axis_index(BLK) * t + jnp.arange(t, dtype=jnp.int32)
    positions = stretch_start[0] + token
    temper = jnp.log(((positions + 1) // 8192).astype(F32) + 1.0) * 0.1 + 1.0
    scaled = (
        lax.optimization_barrier(queries).astype(F32) * (temper * d ** (-0.5))[:, None]
    ).astype(BF)

    chunks = ring(scaled, "z")
    chunks, caches, lens = lax.optimization_barrier((chunks, caches, lens))
    partial = attend(lens, where, chunks, list(range(nz)), caches, new_pairs)
    returned = lax.all_to_all(partial, "z", 0, 0, tiled=True)

    out_near = w_out.T
    out_beside = shift(out_near, "y", 1)
    out_four = [out_near, shift(out_near, "c", 1), out_beside, shift(out_beside, "c", 1)]
    returned, out_four = lax.optimization_barrier((returned, out_four))
    context = merge(returned, d)

    terms = project_out(where, ring(context, "z"), out_four)
    summed = lax.all_to_all(terms, "head", 0, 0, tiled=True).astype(F32).sum(axis=0).astype(BF)
    final = lax.all_to_all(summed.reshape(t, 4, -1).transpose(1, 0, 2), ("y", "c"), 0, 0, tiled=True)
    return final.reshape(4 * t, -1)


def solution(mesh):
    finer = Mesh(mesh.devices.reshape(8, 2, 2, mesh.shape["head"]), ("z", "y", "c", "head"))
    return jax.shard_map(
        per_device,
        mesh=finer,
        in_specs=(
            P(BLK, None),
            P(),
            P(BLK, "head"),
            P(BLK, "head"),
            P(BLK, "head"),
            P("head", BLK),
            P("head", BLK, None),
            P("head", BLK, None),
            P(BLK),
            P(),
        ),
        out_specs=P("head", BLK),
        check_vma=False,
    )
```

```python
import functools

import jax
import jax.numpy as jnp
from jax import lax
from jax.experimental import pallas as pl
from jax.experimental.pallas import tpu as pltpu
from jax.sharding import Mesh
from jax.sharding import PartitionSpec as P

BLK = ("z", "y", "c")
BF = jnp.bfloat16
F32 = jnp.float32
NEG = -1e30
KEYS = 512


def shift(x, axis, d):
    n = lax.axis_size(axis)
    return lax.ppermute(x, axis, [(i, (i + d) % n) for i in range(n)])


def ring(x, axis, beside=None):
    n = lax.axis_size(axis)
    ahead, behind = [x], [x]
    for step in range(n // 2):
        if beside and step in beside:
            ahead[-1], beside[step] = lax.optimization_barrier((ahead[-1], beside[step]))
        ahead.append(shift(ahead[-1], axis, 1))
        if step < (n - 1) // 2:
            behind.append(shift(behind[-1], axis, -1))
    return ahead + behind[:0:-1]


def nt(a, b):
    return lax.dot_general(a, b, (((1,), (1,)), ((), ())), preferred_element_type=F32)


def tn(a, b):
    return lax.dot_general(a, b, (((0,), (0,)), ((), ())), preferred_element_type=F32)


VM = pl.BlockSpec(memory_space=pltpu.VMEM)
SM = pl.BlockSpec(memory_space=pltpu.SMEM)


def params(mib=56):
    return pltpu.CompilerParams(vmem_limit_bytes=mib << 20)


def side_by_side(arrays):
    rows = arrays[0].shape[0]
    widths = [a.shape[1] for a in arrays]

    def body(*refs):
        out, at = refs[-1], 0
        for ref, width in zip(refs[:-1], widths):
            out[:, at : at + width] = ref[...]
            at += width

    return pl.pallas_call(
        body,
        out_shape=jax.ShapeDtypeStruct((rows, sum(widths)), arrays[0].dtype),
        in_specs=[VM] * len(arrays),
        out_specs=VM,
        compiler_params=params(),
        name="side_by_side",
    )(*arrays)


def project(where, x, blocks):
    rows, _ = x.shape
    n = len(blocks)
    r, cols = blocks[0].shape
    t = rows // 4

    def kernel(where_ref, x_ref, *refs):
        w_refs, (keep, send, whole, total) = refs[:n], refs[n:]
        z, c = where_ref[0], where_ref[2]
        for d in range(n):
            at = lax.rem(z + (n - d), n)
            whole[pl.ds(pl.multiple_of(at * r, 16), r), :] = w_refs[d][...]
        total[...] = jnp.dot(x_ref[...], whole[...], preferred_element_type=F32).reshape(4, t, cols)
        for y in range(2):
            keep[y] = total[2 * y + c]
            send[y] = total[2 * y + 1 - c]

    half = jax.ShapeDtypeStruct((2, t, cols), F32)
    return pl.pallas_call(
        kernel,
        out_shape=[half, half],
        in_specs=[SM, VM] + [VM] * n,
        out_specs=[VM, VM],
        scratch_shapes=[pltpu.VMEM((n * r, cols), BF), pltpu.VMEM((4, t, cols), F32)],
        compiler_params=params(),
        name="project",
    )(where, x, *blocks)


def sum_cores(where, kept, came, q_cols):
    _, t, cols = kept.shape

    def kernel(where_ref, a_ref, b_ref, near, away, rest):
        y = where_ref[1]
        near[...] = a_ref[y, :, :q_cols] + b_ref[y, :, :q_cols]
        away[...] = a_ref[1 - y, :, :q_cols] + b_ref[1 - y, :, :q_cols]
        rest[...] = a_ref[:, :, q_cols:] + b_ref[:, :, q_cols:]

    q = jax.ShapeDtypeStruct((t, q_cols), F32)
    return pl.pallas_call(
        kernel,
        out_shape=[q, q, jax.ShapeDtypeStruct((2, t, cols - q_cols), F32)],
        in_specs=[SM, VM, VM],
        out_specs=[VM, VM, VM],
        compiler_params=params(),
        name="sum_cores",
    )(where, kept, came)


def norm_cut(hidden, gain, n):
    t, model = hidden.shape
    width = model // (4 * n)

    def kernel(h_ref, g_ref, out):
        x = h_ref[...].astype(F32)
        normed = (
            x * lax.rsqrt(jnp.mean(x * x, axis=-1, keepdims=True) + 1e-05) * g_ref[...]
        ).astype(BF)
        for k in range(n):
            for j in range(4):
                at = (4 * k + j) * width
                out[j, :, k * width : (k + 1) * width] = normed[:, at : at + width]

    return pl.pallas_call(
        kernel,
        out_shape=jax.ShapeDtypeStruct((4, t, n * width), BF),
        in_specs=[VM, VM],
        out_specs=VM,
        compiler_params=params(),
        name="norm_cut",
    )(hidden, gain.reshape(1, model))


TAIL = 16


def join_cache(keys, values, length):
    rows, d = keys.shape

    def kernel(len_ref, k_ref, v_ref, out):
        out[0:rows, :] = k_ref[...]
        out[rows : 2 * rows, :] = v_ref[...]
        lane = lax.broadcasted_iota(jnp.int32, (TAIL, d), 1)
        digits = jnp.where(lane == 0, len_ref[0] // 64, lax.rem(len_ref[0], 64))
        out[2 * rows :, :] = digits.astype(F32).astype(BF)

    return pl.pallas_call(
        kernel,
        out_shape=jax.ShapeDtypeStruct((2 * rows + TAIL, d), keys.dtype),
        in_specs=[SM, VM, VM],
        out_specs=VM,
        compiler_params=params(),
        name="join_cache",
    )(length, keys, values)


def attend(where, chunks, dists, caches, new_pairs):
    n = len(chunks)
    t, width = chunks[0].shape
    d = caches[0].shape[1]
    each = (caches[0].shape[0] - TAIL) // 2
    ns = len(caches)
    room = ns * each + 4 * KEYS
    g = width // d
    rows = n * g * t
    fresh = new_pairs[0][0].shape[0]

    def kernel(where_ref, *refs):
        q_refs = refs[:n]
        c_refs = refs[n : n + ns]
        nk0, nv0, nk1, nv1 = refs[n + ns : n + ns + 4]
        out = refs[n + ns + 4]
        q_all, m, l, acc, s_a, s_b, token, stats, k_ref, v_ref = refs[n + ns + 5 :]
        top_key = c_refs[0][0:1, :]
        at = jnp.int32(0)
        counted = jnp.int32(0)
        lane = lax.broadcasted_iota(jnp.int32, (TAIL, d), 1)
        row = lax.broadcasted_iota(jnp.int32, (TAIL, d), 0)
        place = jnp.where(row > 0, 0.0, jnp.where(lane == 0, 64.0, jnp.where(lane == 1, 1.0, 0.0)))
        for i in range(ns):
            digits = c_refs[i][2 * each : 2 * each + TAIL, :].astype(F32)
            length = jnp.sum(digits * place).astype(jnp.int32)
            counted = counted + length
            at = pl.multiple_of(at, 16)
            k_ref[pl.ds(at, each), :] = c_refs[i][0:each, :]
            v_ref[pl.ds(at, each), :] = c_refs[i][each : 2 * each, :]
            whole = length // 16
            odd = length - whole * 16
            tail = pl.multiple_of(at + whole * 16, 16)

            @pl.when(odd > 0)
            def _():
                valid = lax.broadcasted_iota(jnp.int32, (16, d), 0) < odd
                k_tile = k_ref[pl.ds(tail, 16), :].astype(F32)
                v_tile = v_ref[pl.ds(tail, 16), :].astype(F32)
                k_ref[pl.ds(tail, 16), :] = jnp.where(valid, k_tile, top_key.astype(F32)).astype(BF)
                v_ref[pl.ds(tail, 16), :] = jnp.where(valid, v_tile, 0.0).astype(BF)

            at = at + ((length + 15) // 16) * 16
        used = pl.multiple_of(at, 16)
        k_ref[pl.ds(used, 2 * KEYS), :] = jnp.broadcast_to(top_key, (2 * KEYS, d))
        v_ref[pl.ds(used, 2 * KEYS), :] = jnp.zeros((2 * KEYS, d), BF)
        z, y, c = where_ref[0], where_ref[1], where_ref[2]
        nz = where_ref[3]
        for i in range(n):
            base = lax.rem(z + nz - dists[i], nz) * (4 * t) + (2 * y + c) * t
            for h in range(g):
                at = (i * g + h) * t
                q_all[at : at + t, :] = q_refs[i][:, h * d : (h + 1) * d]
            span = slice(i * g * t, (i + 1) * g * t)
            token[:, span] = base + lax.rem(lax.broadcasted_iota(jnp.int32, (1, g * t), 1), t)
        m[...] = jnp.full(m.shape, NEG, F32)
        l[...] = jnp.zeros(l.shape, F32)
        acc[...] = jnp.zeros(acc.shape, F32)

        def scores(at):
            return nt(k_ref[pl.ds(pl.multiple_of(at, KEYS), KEYS), :], q_all[...])

        def absorb(s, values):
            before = m[...]
            now = jnp.maximum(before, jnp.max(s, axis=0, keepdims=True))
            fade = jnp.exp(before - now)
            p = jnp.exp(s - now)
            l[...] = l[...] * fade + jnp.sum(p, axis=0, keepdims=True)
            m[...] = now
            acc[...] = acc[...] * fade + tn(values, p.astype(BF))

        def values_at(at):
            return v_ref[pl.ds(pl.multiple_of(at, KEYS), KEYS), :]

        pairs = (used + 2 * KEYS - 1) // (2 * KEYS)
        s_a[...] = scores(0)

        def visit(u, _):
            at = u * (2 * KEYS)
            s_b[...] = scores(at + KEYS)
            absorb(s_a[...], values_at(at))
            s_a[...] = scores(at + 2 * KEYS)
            absorb(s_b[...], values_at(at + KEYS))
            return 0

        lax.fori_loop(0, pairs, visit, 0)
        extra = (pairs * (2 * KEYS) - counted).astype(F32)
        first = nt(k_ref[0:8, :], q_all[...])[0:1]
        l[...] = l[...] - extra * jnp.exp(first - m[...])
        for part, (nk, nv) in enumerate(((nk0, nv0), (nk1, nv1))):
            row = lax.broadcasted_iota(jnp.int32, (fresh, 1), 0)
            side = c if part == 0 else 1 - c
            key_token = z * (4 * t) + (row // t) * (2 * t) + side * t + lax.rem(row, t)
            s = nt(nk[...], q_all[...])
            s = jnp.where(key_token <= token[...], s, NEG)
            absorb(s, nv[...])
        top = m[...]
        top_hi = top.astype(BF).astype(F32)
        top_lo = (top - top_hi).astype(BF).astype(F32)
        scale = jnp.exp(top - (top_hi + top_lo))
        den = l[...] * scale
        den_hi = den.astype(BF).astype(F32)
        den_lo = den - den_hi
        numer = (acc[...] * scale).T
        stats[...] = jnp.zeros(stats.shape, F32)
        for i in range(n):
            owner = lax.rem(z + nz - dists[i], nz)
            for h in range(g):
                at = slice((i * g + h) * t, (i * g + h + 1) * t)
                out[owner, :, h * d : (h + 1) * d] = numer[at].astype(BF)
                for k, row in enumerate((top_hi, top_lo, den_hi, den_lo)):
                    stats[8 * k + h : 8 * k + h + 1, :] = row[:, at]
            out[owner, :, g * d :] = stats[...].T.astype(BF)

    return pl.pallas_call(
        kernel,
        out_shape=jax.ShapeDtypeStruct((n, t, width + 128), BF),
        in_specs=[SM] + [VM] * (n + ns + 4),
        out_specs=VM,
        scratch_shapes=[
            pltpu.VMEM((rows, d), BF),
            pltpu.VMEM((1, rows), F32),
            pltpu.VMEM((1, rows), F32),
            pltpu.VMEM((d, rows), F32),
            pltpu.VMEM((KEYS, rows), F32),
            pltpu.VMEM((KEYS, rows), F32),
            pltpu.VMEM((1, rows), jnp.int32),
            pltpu.VMEM((128, t), F32),
            pltpu.VMEM((room, d), BF),
            pltpu.VMEM((room, d), BF),
        ],
        compiler_params=params(),
        name="attend",
    )(where, *chunks, *caches, *new_pairs[0], *new_pairs[1])


def merge(parts, d):
    n, t, width = parts.shape
    g = (width - 128) // d

    def kernel(ins, out):
        stats = [ins[i, :, g * d :].astype(F32) for i in range(n)]
        for h in range(g):
            tops = [s[:, h : h + 1] + s[:, 8 + h : 9 + h] for s in stats]
            dens = [s[:, 16 + h : 17 + h] + s[:, 24 + h : 25 + h] for s in stats]
            top = functools.reduce(jnp.maximum, tops)
            shares = [jnp.exp(a - top) for a in tops]
            den = sum(w * a for w, a in zip(shares, dens))
            num = sum(w * ins[i, :, h * d : (h + 1) * d].astype(F32) for i, w in enumerate(shares))
            out[:, h * d : (h + 1) * d] = (num / den).astype(BF)

    return pl.pallas_call(
        kernel,
        out_shape=jax.ShapeDtypeStruct((t, g * d), BF),
        in_specs=[VM],
        out_specs=VM,
        compiler_params=params(),
        name="merge",
    )(parts)


def project_out(where, contexts, weights):
    n = len(contexts)
    t, inner = contexts[0].shape
    cols = weights[0].shape[0]

    def kernel(where_ref, *refs):
        c_refs, w_refs = refs[:n], refs[n : n + 4]
        out, tokens, w_all = refs[n + 4 :]
        z, here = where_ref[0], 2 * where_ref[1] + where_ref[2]
        for i in range(n):
            tokens[lax.rem(z + (n - i), n)] = c_refs[i][...]
        for f in range(4):
            w_all[f ^ here] = w_refs[f][...]
        res = nt(tokens[...].reshape(n * t, inner), w_all[...].reshape(4 * cols, inner))
        out[...] = res.astype(BF).reshape(n, t, 4 * cols)

    return pl.pallas_call(
        kernel,
        out_shape=jax.ShapeDtypeStruct((n, t, 4 * cols), BF),
        in_specs=[SM] + [VM] * (n + 4),
        out_specs=VM,
        scratch_shapes=[
            pltpu.VMEM((n, t, inner), BF),
            pltpu.VMEM((4, cols, inner), BF),
        ],
        compiler_params=params(),
        name="project_out",
    )(where, *contexts, *weights)


def per_device(
    hidden,
    norm_gain,
    w_query,
    key_projection_weight,
    value_projection_weight,
    w_out,
    cache_keys,
    earlier_values,
    cache_len,
    stretch_start,
):
    t, model = hidden.shape
    d = cache_keys.shape[2]
    q_cols = w_query.shape[1]
    kv_cols = key_projection_weight.shape[1]
    nz = lax.axis_size("z")
    z, y, c = lax.axis_index("z"), lax.axis_index("y"), lax.axis_index("c")
    where = jnp.stack([z, y, c, jnp.int32(nz)]).astype(jnp.int32)

    cut = norm_cut(hidden, norm_gain, nz)
    x = lax.all_to_all(cut, ("y", "c"), 0, 0, tiled=True).reshape(4 * t, model // 4)
    near = join_cache(cache_keys[0], earlier_values[0], cache_len)

    weights = side_by_side([w_query, key_projection_weight, value_projection_weight])
    beside = {1: near, 2: x}
    blocks = ring(weights, "z", beside)
    near, x = beside[1], beside[2]

    beside = shift(near, "y", 1)
    x, beside = lax.optimization_barrier((x, beside))
    caches = [near, beside, shift(near, "c", 1), shift(beside, "c", 1)]

    keep, send = project(where, x, blocks)
    q_near, q_away, kv = sum_cores(where, keep, shift(send, "c", 1), q_cols)
    queries = (q_near + shift(q_away, "y", 1)).astype(BF)
    fresh = (kv + shift(kv, "y", 1)).astype(BF).reshape(2 * t, 2 * kv_cols)
    other = shift(fresh, "c", 1)
    new_pairs = [(f[:, :kv_cols], f[:, kv_cols:]) for f in (fresh, other)]

    token = lax.axis_index(BLK) * t + jnp.arange(t, dtype=jnp.int32)
    positions = stretch_start[0] + token
    temper = jnp.log(((positions + 1) // 8192).astype(F32) + 1.0) * 0.1 + 1.0
    scaled = (
        lax.optimization_barrier(queries).astype(F32) * (temper * d ** (-0.5))[:, None]
    ).astype(BF)

    chunks = ring(scaled, "z")
    chunks, caches = lax.optimization_barrier((chunks, caches))
    partial = attend(where, chunks, list(range(nz)), caches, new_pairs)
    returned = lax.all_to_all(partial, "z", 0, 0, tiled=True)

    out_near = w_out.T
    out_beside = shift(out_near, "y", 1)
    out_four = [out_near, shift(out_near, "c", 1), out_beside, shift(out_beside, "c", 1)]
    returned, out_four = lax.optimization_barrier((returned, out_four))
    context = merge(returned, d)

    terms = project_out(where, ring(context, "z"), out_four)
    summed = lax.all_to_all(terms, "head", 0, 0, tiled=True).astype(F32).sum(axis=0).astype(BF)
    final = lax.all_to_all(summed.reshape(t, 4, -1).transpose(1, 0, 2), ("y", "c"), 0, 0, tiled=True)
    return final.reshape(4 * t, -1)


def solution(mesh):
    finer = Mesh(mesh.devices.reshape(8, 2, 2, mesh.shape["head"]), ("z", "y", "c", "head"))
    return jax.shard_map(
        per_device,
        mesh=finer,
        in_specs=(
            P(BLK, None),
            P(),
            P(BLK, "head"),
            P(BLK, "head"),
            P(BLK, "head"),
            P("head", BLK),
            P("head", BLK, None),
            P("head", BLK, None),
            P(BLK),
            P(),
        ),
        out_specs=P("head", BLK),
        check_vma=False,
    )
```

```python
import functools

import jax
import jax.numpy as jnp
from jax import lax
from jax.experimental import pallas as pl
from jax.experimental.pallas import tpu as pltpu
from jax.sharding import Mesh
from jax.sharding import PartitionSpec as P

BLK = ("z", "y", "c")
BF = jnp.bfloat16
F32 = jnp.float32
NEG = -1e30
KEYS = 512


def shift(x, axis, d):
    n = lax.axis_size(axis)
    return lax.ppermute(x, axis, [(i, (i + d) % n) for i in range(n)])


def ring(x, axis, beside=None):
    n = lax.axis_size(axis)
    ahead, behind = [x], [x]
    for step in range(n // 2):
        if beside and step in beside:
            ahead[-1], beside[step] = lax.optimization_barrier((ahead[-1], beside[step]))
        ahead.append(shift(ahead[-1], axis, 1))
        if step < (n - 1) // 2:
            behind.append(shift(behind[-1], axis, -1))
        if beside and step == 0:
            ahead[-1], behind[-1] = lax.optimization_barrier((ahead[-1], behind[-1]))
    return ahead + behind[:0:-1]


def nt(a, b):
    return lax.dot_general(a, b, (((1,), (1,)), ((), ())), preferred_element_type=F32)


def tn(a, b):
    return lax.dot_general(a, b, (((0,), (0,)), ((), ())), preferred_element_type=F32)


VM = pl.BlockSpec(memory_space=pltpu.VMEM)
SM = pl.BlockSpec(memory_space=pltpu.SMEM)


def params(mib=56):
    return pltpu.CompilerParams(vmem_limit_bytes=mib << 20)


def side_by_side(arrays):
    rows = arrays[0].shape[0]
    widths = [a.shape[1] for a in arrays]

    def body(*refs):
        out, at = refs[-1], 0
        for ref, width in zip(refs[:-1], widths):
            out[:, at : at + width] = ref[...]
            at += width

    return pl.pallas_call(
        body,
        out_shape=jax.ShapeDtypeStruct((rows, sum(widths)), arrays[0].dtype),
        in_specs=[VM] * len(arrays),
        out_specs=VM,
        compiler_params=params(),
        name="side_by_side",
    )(*arrays)


def project(where, x, blocks):
    rows, _ = x.shape
    n = len(blocks)
    r, cols = blocks[0].shape
    t = rows // 4

    def kernel(where_ref, x_ref, *refs):
        w_refs, (keep, send, whole, total) = refs[:n], refs[n:]
        z, c = where_ref[0], where_ref[2]
        for d in range(n):
            at = lax.rem(z + (n - d), n)
            whole[pl.ds(pl.multiple_of(at * r, 16), r), :] = w_refs[d][...]
        total[...] = jnp.dot(x_ref[...], whole[...], preferred_element_type=F32).reshape(4, t, cols)
        for y in range(2):
            keep[y] = total[2 * y + c]
            send[y] = total[2 * y + 1 - c]

    half = jax.ShapeDtypeStruct((2, t, cols), F32)
    return pl.pallas_call(
        kernel,
        out_shape=[half, half],
        in_specs=[SM, VM] + [VM] * n,
        out_specs=[VM, VM],
        scratch_shapes=[pltpu.VMEM((n * r, cols), BF), pltpu.VMEM((4, t, cols), F32)],
        compiler_params=params(),
        name="project",
    )(where, x, *blocks)


def sum_cores(where, kept, came, q_cols):
    _, t, cols = kept.shape

    def kernel(where_ref, a_ref, b_ref, near, away, rest):
        y = where_ref[1]
        near[...] = a_ref[y, :, :q_cols] + b_ref[y, :, :q_cols]
        away[...] = a_ref[1 - y, :, :q_cols] + b_ref[1 - y, :, :q_cols]
        rest[...] = a_ref[:, :, q_cols:] + b_ref[:, :, q_cols:]

    q = jax.ShapeDtypeStruct((t, q_cols), F32)
    return pl.pallas_call(
        kernel,
        out_shape=[q, q, jax.ShapeDtypeStruct((2, t, cols - q_cols), F32)],
        in_specs=[SM, VM, VM],
        out_specs=[VM, VM, VM],
        compiler_params=params(),
        name="sum_cores",
    )(where, kept, came)


def norm_cut(hidden, gain, n):
    t, model = hidden.shape
    width = model // (4 * n)

    def kernel(h_ref, g_ref, out):
        x = h_ref[...].astype(F32)
        normed = (
            x * lax.rsqrt(jnp.mean(x * x, axis=-1, keepdims=True) + 1e-05) * g_ref[...]
        ).astype(BF)
        for k in range(n):
            for j in range(4):
                at = (4 * k + j) * width
                out[j, :, k * width : (k + 1) * width] = normed[:, at : at + width]

    return pl.pallas_call(
        kernel,
        out_shape=jax.ShapeDtypeStruct((4, t, n * width), BF),
        in_specs=[VM, VM],
        out_specs=VM,
        compiler_params=params(),
        name="norm_cut",
    )(hidden, gain.reshape(1, model))


TAIL = 16


def join_cache(keys, values, length):
    rows, d = keys.shape

    def kernel(len_ref, k_ref, v_ref, out):
        out[0:rows, :] = k_ref[...]
        out[rows : 2 * rows, :] = v_ref[...]
        lane = lax.broadcasted_iota(jnp.int32, (TAIL, d), 1)
        digits = jnp.where(lane == 0, len_ref[0] // 64, lax.rem(len_ref[0], 64))
        out[2 * rows :, :] = digits.astype(F32).astype(BF)

    return pl.pallas_call(
        kernel,
        out_shape=jax.ShapeDtypeStruct((2 * rows + TAIL, d), keys.dtype),
        in_specs=[SM, VM, VM],
        out_specs=VM,
        compiler_params=params(),
        name="join_cache",
    )(length, keys, values)


def attend(where, chunks, dists, caches, new_pairs):
    n = len(chunks)
    t, width = chunks[0].shape
    d = caches[0].shape[1]
    each = (caches[0].shape[0] - TAIL) // 2
    ns = len(caches)
    room = ns * each + 4 * KEYS
    g = width // d
    rows = n * g * t
    fresh = new_pairs[0][0].shape[0]

    def kernel(where_ref, *refs):
        q_refs = refs[:n]
        c_refs = refs[n : n + ns]
        nk0, nv0, nk1, nv1 = refs[n + ns : n + ns + 4]
        out = refs[n + ns + 4]
        q_all, m, l, acc, s_a, s_b, token, stats, k_ref, v_ref = refs[n + ns + 5 :]
        top_key = c_refs[0][0:1, :]
        at = jnp.int32(0)
        counted = jnp.int32(0)
        lane = lax.broadcasted_iota(jnp.int32, (TAIL, d), 1)
        row = lax.broadcasted_iota(jnp.int32, (TAIL, d), 0)
        place = jnp.where(row > 0, 0.0, jnp.where(lane == 0, 64.0, jnp.where(lane == 1, 1.0, 0.0)))
        for i in range(ns):
            digits = c_refs[i][2 * each : 2 * each + TAIL, :].astype(F32)
            length = jnp.sum(digits * place).astype(jnp.int32)
            counted = counted + length
            at = pl.multiple_of(at, 16)
            k_ref[pl.ds(at, each), :] = c_refs[i][0:each, :]
            v_ref[pl.ds(at, each), :] = c_refs[i][each : 2 * each, :]
            whole = length // 16
            odd = length - whole * 16
            tail = pl.multiple_of(at + whole * 16, 16)

            @pl.when(odd > 0)
            def _():
                valid = lax.broadcasted_iota(jnp.int32, (16, d), 0) < odd
                k_tile = k_ref[pl.ds(tail, 16), :].astype(F32)
                v_tile = v_ref[pl.ds(tail, 16), :].astype(F32)
                k_ref[pl.ds(tail, 16), :] = jnp.where(valid, k_tile, top_key.astype(F32)).astype(BF)
                v_ref[pl.ds(tail, 16), :] = jnp.where(valid, v_tile, 0.0).astype(BF)

            at = at + ((length + 15) // 16) * 16
        used = pl.multiple_of(at, 16)
        k_ref[pl.ds(used, 2 * KEYS), :] = jnp.broadcast_to(top_key, (2 * KEYS, d))
        v_ref[pl.ds(used, 2 * KEYS), :] = jnp.zeros((2 * KEYS, d), BF)
        z, y, c = where_ref[0], where_ref[1], where_ref[2]
        nz = where_ref[3]
        for i in range(n):
            base = lax.rem(z + nz - dists[i], nz) * (4 * t) + (2 * y + c) * t
            for h in range(g):
                at = (i * g + h) * t
                q_all[at : at + t, :] = q_refs[i][:, h * d : (h + 1) * d]
            span = slice(i * g * t, (i + 1) * g * t)
            token[:, span] = base + lax.rem(lax.broadcasted_iota(jnp.int32, (1, g * t), 1), t)
        m[...] = jnp.full(m.shape, NEG, F32)
        l[...] = jnp.zeros(l.shape, F32)
        acc[...] = jnp.zeros(acc.shape, F32)

        def scores(at):
            return nt(k_ref[pl.ds(pl.multiple_of(at, KEYS), KEYS), :], q_all[...])

        def absorb(s, values):
            before = m[...]
            now = jnp.maximum(before, jnp.max(s, axis=0, keepdims=True))
            fade = jnp.exp(before - now)
            p = jnp.exp(s - now)
            l[...] = l[...] * fade + jnp.sum(p, axis=0, keepdims=True)
            m[...] = now
            acc[...] = acc[...] * fade + tn(values, p.astype(BF))

        def values_at(at):
            return v_ref[pl.ds(pl.multiple_of(at, KEYS), KEYS), :]

        pairs = (used + 2 * KEYS - 1) // (2 * KEYS)
        s_a[...] = scores(0)

        def visit(u, _):
            at = u * (2 * KEYS)
            s_b[...] = scores(at + KEYS)
            absorb(s_a[...], values_at(at))
            s_a[...] = scores(at + 2 * KEYS)
            absorb(s_b[...], values_at(at + KEYS))
            return 0

        lax.fori_loop(0, pairs, visit, 0)
        extra = (pairs * (2 * KEYS) - counted).astype(F32)
        first = nt(k_ref[0:8, :], q_all[...])[0:1]
        l[...] = l[...] - extra * jnp.exp(first - m[...])
        for part, (nk, nv) in enumerate(((nk0, nv0), (nk1, nv1))):
            row = lax.broadcasted_iota(jnp.int32, (fresh, 1), 0)
            side = c if part == 0 else 1 - c
            key_token = z * (4 * t) + (row // t) * (2 * t) + side * t + lax.rem(row, t)
            s = nt(nk[...], q_all[...])
            s = jnp.where(key_token <= token[...], s, NEG)
            absorb(s, nv[...])
        top = m[...]
        top_hi = top.astype(BF).astype(F32)
        top_lo = (top - top_hi).astype(BF).astype(F32)
        scale = jnp.exp(top - (top_hi + top_lo))
        den = l[...] * scale
        den_hi = den.astype(BF).astype(F32)
        den_lo = den - den_hi
        numer = (acc[...] * scale).T
        stats[...] = jnp.zeros(stats.shape, F32)
        for i in range(n):
            owner = lax.rem(z + nz - dists[i], nz)
            for h in range(g):
                at = slice((i * g + h) * t, (i * g + h + 1) * t)
                out[:, owner, :, h * d : (h + 1) * d] = numer[at].reshape(n, t // n, d).astype(BF)
                for k, row in enumerate((top_hi, top_lo, den_hi, den_lo)):
                    stats[8 * k + h : 8 * k + h + 1, :] = row[:, at]
            out[:, owner, :, g * d :] = stats[...].T.reshape(n, t // n, 128).astype(BF)

    return pl.pallas_call(
        kernel,
        out_shape=jax.ShapeDtypeStruct((n, n, t // n, width + 128), BF),
        in_specs=[SM] + [VM] * (n + ns + 4),
        out_specs=VM,
        scratch_shapes=[
            pltpu.VMEM((rows, d), BF),
            pltpu.VMEM((1, rows), F32),
            pltpu.VMEM((1, rows), F32),
            pltpu.VMEM((d, rows), F32),
            pltpu.VMEM((KEYS, rows), F32),
            pltpu.VMEM((KEYS, rows), F32),
            pltpu.VMEM((1, rows), jnp.int32),
            pltpu.VMEM((128, t), F32),
            pltpu.VMEM((room, d), BF),
            pltpu.VMEM((room, d), BF),
        ],
        compiler_params=params(),
        name="attend",
    )(where, *chunks, *caches, *new_pairs[0], *new_pairs[1])


def merge(parts, d):
    n, t, width = parts.shape
    g = (width - 128) // d

    def kernel(ins, out):
        stats = [ins[i, :, g * d :].astype(F32) for i in range(n)]
        for h in range(g):
            tops = [s[:, h : h + 1] + s[:, 8 + h : 9 + h] for s in stats]
            dens = [s[:, 16 + h : 17 + h] + s[:, 24 + h : 25 + h] for s in stats]
            top = functools.reduce(jnp.maximum, tops)
            shares = [jnp.exp(a - top) for a in tops]
            den = sum(w * a for w, a in zip(shares, dens))
            num = sum(w * ins[i, :, h * d : (h + 1) * d].astype(F32) for i, w in enumerate(shares))
            out[:, h * d : (h + 1) * d] = (num / den).astype(BF)

    return pl.pallas_call(
        kernel,
        out_shape=jax.ShapeDtypeStruct((t, g * d), BF),
        in_specs=[VM],
        out_specs=VM,
        compiler_params=params(),
        name="merge",
    )(parts)


def project_out(where, contexts, weights, n):
    t, inner = contexts[0].shape
    cols = weights.shape[0]
    part = t // n

    def kernel(where_ref, *refs):
        c_refs, (w_ref, out, tokens) = refs[:4], refs[4:]
        here = 2 * where_ref[1] + where_ref[2]
        for f in range(4):
            tokens[:, f ^ here] = c_refs[f][...].reshape(n, part, inner).astype(F32)
        rows = tokens[...].reshape(4 * t, inner).astype(BF)
        out[...] = nt(rows, w_ref[...]).astype(BF).reshape(n, 4 * part, cols)

    return pl.pallas_call(
        kernel,
        out_shape=jax.ShapeDtypeStruct((n, 4 * part, cols), BF),
        in_specs=[SM] + [VM] * 5,
        out_specs=VM,
        scratch_shapes=[pltpu.VMEM((n, 4, part, inner), F32)],
        compiler_params=params(),
        name="project_out",
    )(where, *contexts, weights)


def sum_heads(parts, n):
    heads, rows, cols = parts.shape
    width = cols // n

    def kernel(p_ref, out):
        total = p_ref[0].astype(F32)
        for i in range(1, heads):
            total = total + p_ref[i].astype(F32)
        for k in range(n):
            out[k] = total[:, k * width : (k + 1) * width].astype(BF)

    return pl.pallas_call(
        kernel,
        out_shape=jax.ShapeDtypeStruct((n, rows, width), BF),
        in_specs=[VM],
        out_specs=VM,
        compiler_params=params(),
        name="sum_heads",
    )(parts)


def per_device(
    hidden,
    norm_gain,
    w_query,
    key_projection_weight,
    value_projection_weight,
    w_out,
    cache_keys,
    earlier_values,
    cache_len,
    stretch_start,
):
    t, model = hidden.shape
    d = cache_keys.shape[2]
    q_cols = w_query.shape[1]
    kv_cols = key_projection_weight.shape[1]
    nz = lax.axis_size("z")
    z, y, c = lax.axis_index("z"), lax.axis_index("y"), lax.axis_index("c")
    where = jnp.stack([z, y, c, jnp.int32(nz)]).astype(jnp.int32)

    cut = norm_cut(hidden, norm_gain, nz)
    x = lax.all_to_all(cut, ("y", "c"), 0, 0, tiled=True).reshape(4 * t, model // 4)
    near = join_cache(cache_keys[0], earlier_values[0], cache_len)

    weights = side_by_side([w_query, key_projection_weight, value_projection_weight])
    beside = {1: near, 2: x}
    blocks = ring(weights, "z", beside)
    near, x = beside[1], beside[2]

    beside = shift(near, "y", 1)
    x, beside = lax.optimization_barrier((x, beside))
    caches = [near, beside, shift(near, "c", 1), shift(beside, "c", 1)]

    keep, send = project(where, x, blocks)
    out_cols, keep = lax.optimization_barrier((w_out.T, keep))
    out_cols = lax.all_gather(out_cols, "z", axis=0, tiled=True)

    q_near, q_away, kv = sum_cores(where, keep, shift(send, "c", 1), q_cols)
    queries = (q_near + shift(q_away, "y", 1)).astype(BF)
    fresh = (kv + shift(kv, "y", 1)).astype(BF).reshape(2 * t, 2 * kv_cols)
    other = shift(fresh, "c", 1)
    new_pairs = [(f[:, :kv_cols], f[:, kv_cols:]) for f in (fresh, other)]

    token = lax.axis_index(BLK) * t + jnp.arange(t, dtype=jnp.int32)
    positions = stretch_start[0] + token
    temper = jnp.log(((positions + 1) // 8192).astype(F32) + 1.0) * 0.1 + 1.0
    scaled = (
        lax.optimization_barrier(queries).astype(F32) * (temper * d ** (-0.5))[:, None]
    ).astype(BF)

    chunks = ring(scaled, "z")
    chunks, caches = lax.optimization_barrier((chunks, caches))
    partial = attend(where, chunks, list(range(nz)), caches, new_pairs)
    returned = lax.all_to_all(partial, "z", 0, 0, tiled=True)
    context = merge(returned.reshape(nz, t, -1), d)
    context_y = shift(context, "y", 1)
    contexts = [context, shift(context, "c", 1), context_y, shift(context_y, "c", 1)]
    terms = project_out(where, contexts, out_cols, nz)
    shares = lax.all_to_all(terms, "head", 0, 0, tiled=True)
    final = lax.all_to_all(sum_heads(shares, nz), "z", 0, 0, tiled=True)
    final = final.reshape(nz, 4, t // nz, -1).transpose(1, 0, 2, 3)
    return final.reshape(4 * t, -1)


def solution(mesh):
    finer = Mesh(mesh.devices.reshape(8, 2, 2, mesh.shape["head"]), ("z", "y", "c", "head"))
    return jax.shard_map(
        per_device,
        mesh=finer,
        in_specs=(
            P(BLK, None),
            P(),
            P(BLK, "head"),
            P(BLK, "head"),
            P(BLK, "head"),
            P("head", BLK),
            P("head", BLK, None),
            P("head", BLK, None),
            P(BLK),
            P(),
        ),
        out_specs=P("head", BLK),
        check_vma=False,
    )
```

```python
import functools

import jax
import jax.numpy as jnp
from jax import lax
from jax.experimental import pallas as pl
from jax.experimental.pallas import tpu as pltpu
from jax.sharding import Mesh
from jax.sharding import PartitionSpec as P

BLK = ("z", "y", "c")
BF = jnp.bfloat16
F32 = jnp.float32
NEG = -1e30
KEYS = 512
SPAN = 256


def shift(x, axis, d):
    n = lax.axis_size(axis)
    return lax.ppermute(x, axis, [(i, (i + d) % n) for i in range(n)])


def ring(x, axis, beside=None):
    n = lax.axis_size(axis)
    ahead, behind = [x], [x]
    for step in range(n // 2):
        if beside and step in beside:
            ahead[-1], beside[step] = lax.optimization_barrier((ahead[-1], beside[step]))
        ahead.append(shift(ahead[-1], axis, 1))
        if step < (n - 1) // 2:
            behind.append(shift(behind[-1], axis, -1))
        if beside and step == 0:
            ahead[-1], behind[-1] = lax.optimization_barrier((ahead[-1], behind[-1]))
    return ahead + behind[:0:-1]


def nt(a, b):
    return lax.dot_general(a, b, (((1,), (1,)), ((), ())), preferred_element_type=F32)


def tn(a, b):
    return lax.dot_general(a, b, (((0,), (0,)), ((), ())), preferred_element_type=F32)


VM = pl.BlockSpec(memory_space=pltpu.VMEM)
SM = pl.BlockSpec(memory_space=pltpu.SMEM)


def params(mib=56):
    return pltpu.CompilerParams(vmem_limit_bytes=mib << 20)


def side_by_side(arrays):
    rows = arrays[0].shape[0]
    widths = [a.shape[1] for a in arrays]

    def body(*refs):
        out, at = refs[-1], 0
        for ref, width in zip(refs[:-1], widths):
            out[:, at : at + width] = ref[...]
            at += width

    return pl.pallas_call(
        body,
        out_shape=jax.ShapeDtypeStruct((rows, sum(widths)), arrays[0].dtype),
        in_specs=[VM] * len(arrays),
        out_specs=VM,
        compiler_params=params(),
        name="side_by_side",
    )(*arrays)


def project(where, x, blocks):
    rows, _ = x.shape
    n = len(blocks)
    r, cols = blocks[0].shape
    t = rows // 4

    def kernel(where_ref, x_ref, *refs):
        w_refs, (keep, send, whole, total) = refs[:n], refs[n:]
        z, c = where_ref[0], where_ref[2]
        for d in range(n):
            at = lax.rem(z + (n - d), n)
            whole[pl.ds(pl.multiple_of(at * r, 16), r), :] = w_refs[d][...]
        total[...] = jnp.dot(x_ref[...], whole[...], preferred_element_type=F32).reshape(4, t, cols)
        for y in range(2):
            keep[y] = total[2 * y + c]
            send[y] = total[2 * y + 1 - c]

    half = jax.ShapeDtypeStruct((2, t, cols), F32)
    return pl.pallas_call(
        kernel,
        out_shape=[half, half],
        in_specs=[SM, VM] + [VM] * n,
        out_specs=[VM, VM],
        scratch_shapes=[pltpu.VMEM((n * r, cols), BF), pltpu.VMEM((4, t, cols), F32)],
        compiler_params=params(),
        name="project",
    )(where, x, *blocks)


def sum_cores(where, kept, came, q_cols):
    _, t, cols = kept.shape

    def kernel(where_ref, a_ref, b_ref, near, away, rest):
        y = where_ref[1]
        near[...] = a_ref[y, :, :q_cols] + b_ref[y, :, :q_cols]
        away[...] = a_ref[1 - y, :, :q_cols] + b_ref[1 - y, :, :q_cols]
        rest[...] = a_ref[:, :, q_cols:] + b_ref[:, :, q_cols:]

    q = jax.ShapeDtypeStruct((t, q_cols), F32)
    return pl.pallas_call(
        kernel,
        out_shape=[q, q, jax.ShapeDtypeStruct((2, t, cols - q_cols), F32)],
        in_specs=[SM, VM, VM],
        out_specs=[VM, VM, VM],
        compiler_params=params(),
        name="sum_cores",
    )(where, kept, came)


def norm_cut(hidden, gain, n):
    t, model = hidden.shape
    width = model // (4 * n)

    def kernel(h_ref, g_ref, out):
        x = h_ref[...].astype(F32)
        normed = (
            x * lax.rsqrt(jnp.mean(x * x, axis=-1, keepdims=True) + 1e-05) * g_ref[...]
        ).astype(BF)
        for k in range(n):
            for j in range(4):
                at = (4 * k + j) * width
                out[j, :, k * width : (k + 1) * width] = normed[:, at : at + width]

    return pl.pallas_call(
        kernel,
        out_shape=jax.ShapeDtypeStruct((4, t, n * width), BF),
        in_specs=[VM, VM],
        out_specs=VM,
        compiler_params=params(),
        name="norm_cut",
    )(hidden, gain.reshape(1, model))


TAIL = 16


def with_length(keys, length):
    rows, d = keys.shape

    def kernel(len_ref, k_ref, out):
        out[0:rows, :] = k_ref[...]
        lane = lax.broadcasted_iota(jnp.int32, (TAIL, d), 1)
        digits = jnp.where(lane == 0, len_ref[0] // 64, lax.rem(len_ref[0], 64))
        out[rows:, :] = digits.astype(F32).astype(BF)

    return pl.pallas_call(
        kernel,
        out_shape=jax.ShapeDtypeStruct((rows + TAIL, d), keys.dtype),
        in_specs=[SM, VM],
        out_specs=VM,
        compiler_params=params(),
        name="with_length",
    )(length, keys)


def attend(where, chunks, dists, keys, values, new_pairs):
    n = len(chunks)
    t, width = chunks[0].shape
    each, d = values[0].shape
    ns = len(keys)
    room = ns * each + 2 * KEYS
    g = width // d
    rows = n * g * t
    fresh = new_pairs[0][0].shape[0]

    def kernel(where_ref, *refs):
        q_refs = refs[:n]
        k_in, v_in, refs = refs[n : n + ns], refs[n + ns : n + 2 * ns], refs[n + 2 * ns :]
        nk0, nv0, nk1, nv1 = refs[:4]
        out, q_all, m, l, acc, s_a, s_b, token, stats, k_ref, v_ref = refs[4:]
        top_key = k_in[0][0:1, :]
        at = jnp.int32(0)
        counted = jnp.int32(0)
        lane = lax.broadcasted_iota(jnp.int32, (TAIL, d), 1)
        row = lax.broadcasted_iota(jnp.int32, (TAIL, d), 0)
        place = jnp.where(row > 0, 0.0, jnp.where(lane == 0, 64.0, jnp.where(lane == 1, 1.0, 0.0)))
        for i in range(ns):
            digits = k_in[i][each : each + TAIL, :].astype(F32)
            length = jnp.sum(digits * place).astype(jnp.int32)
            counted = counted + length
            at = pl.multiple_of(at, 16)
            k_ref[pl.ds(at, each), :] = k_in[i][0:each, :]
            v_ref[pl.ds(at, each), :] = v_in[i][...]
            whole = length // 16
            odd = length - whole * 16
            tail = pl.multiple_of(at + whole * 16, 16)

            @pl.when(odd > 0)
            def _():
                valid = lax.broadcasted_iota(jnp.int32, (16, d), 0) < odd
                k_tile = k_ref[pl.ds(tail, 16), :].astype(F32)
                v_tile = v_ref[pl.ds(tail, 16), :].astype(F32)
                k_ref[pl.ds(tail, 16), :] = jnp.where(valid, k_tile, top_key.astype(F32)).astype(BF)
                v_ref[pl.ds(tail, 16), :] = jnp.where(valid, v_tile, 0.0).astype(BF)

            at = at + ((length + 15) // 16) * 16
        used = pl.multiple_of(at, 16)
        k_ref[pl.ds(used, KEYS), :] = jnp.broadcast_to(top_key, (KEYS, d))
        v_ref[pl.ds(used, KEYS), :] = jnp.zeros((KEYS, d), BF)
        z, y, c = where_ref[0], where_ref[1], where_ref[2]
        nz = where_ref[3]
        for i in range(n):
            base = lax.rem(z + nz - dists[i], nz) * (4 * t) + (2 * y + c) * t
            for h in range(g):
                at = (i * g + h) * t
                q_all[at : at + t, :] = q_refs[i][:, h * d : (h + 1) * d]
            span = slice(i * g * t, (i + 1) * g * t)
            token[:, span] = base + lax.rem(lax.broadcasted_iota(jnp.int32, (1, g * t), 1), t)
        m[...] = jnp.full(m.shape, NEG, F32)
        l[...] = jnp.zeros(l.shape, F32)
        acc[...] = jnp.zeros(acc.shape, F32)

        def absorb(s, values, cs):
            before = m[:, cs]
            now = jnp.maximum(before, jnp.max(s, axis=0, keepdims=True))
            fade = jnp.exp(before - now)
            p = jnp.exp(s - now)
            l[:, cs] = l[:, cs] * fade + jnp.sum(p, axis=0, keepdims=True)
            m[:, cs] = now
            acc[:, cs] = acc[:, cs] * fade + tn(values, p.astype(BF))

        def block(ref, u):
            return ref[pl.ds(pl.multiple_of(u * KEYS, KEYS), KEYS), :]

        spans = [slice(lo, lo + SPAN) for lo in range(0, rows, SPAN)]
        blocks = (used + KEYS - 1) // KEYS
        for cs in spans:
            s_a[:, cs] = nt(block(k_ref, 0), q_all[cs, :])

        def visit(u, _):
            for now, then, at in ((s_a, s_b, 2 * u), (s_b, s_a, 2 * u + 1)):
                k_next, v_here = block(k_ref, at + 1), block(v_ref, at)
                for cs in spans:
                    then[:, cs] = nt(k_next, q_all[cs, :])
                    absorb(now[:, cs], v_here, cs)
            return 0

        lax.fori_loop(0, blocks // 2, visit, 0)

        @pl.when(lax.rem(blocks, 2) == 1)
        def _():
            v_last = block(v_ref, blocks - 1)
            for cs in spans:
                absorb(s_a[:, cs], v_last, cs)

        extra = (blocks * KEYS - counted).astype(F32)
        first = nt(k_ref[0:8, :], q_all[...])[0:1]
        l[...] = l[...] - extra * jnp.exp(first - m[...])
        for part, (nk, nv) in enumerate(((nk0, nv0), (nk1, nv1))):
            row = lax.broadcasted_iota(jnp.int32, (fresh, 1), 0)
            side = c if part == 0 else 1 - c
            key_token = z * (4 * t) + (row // t) * (2 * t) + side * t + lax.rem(row, t)
            for cs in spans:
                s = nt(nk[...], q_all[cs, :])
                absorb(jnp.where(key_token <= token[:, cs], s, NEG), nv[...], cs)
        top = m[...]
        top_hi = top.astype(BF).astype(F32)
        top_lo = (top - top_hi).astype(BF).astype(F32)
        scale = jnp.exp(top - (top_hi + top_lo))
        den = l[...] * scale
        den_hi = den.astype(BF).astype(F32)
        den_lo = den - den_hi
        numer = (acc[...] * scale).T
        stats[...] = jnp.zeros(stats.shape, F32)
        for i in range(n):
            owner = lax.rem(z + nz - dists[i], nz)
            for h in range(g):
                at = slice((i * g + h) * t, (i * g + h + 1) * t)
                out[:, owner, :, h * d : (h + 1) * d] = numer[at].reshape(n, t // n, d).astype(BF)
                for k, row in enumerate((top_hi, top_lo, den_hi, den_lo)):
                    stats[8 * k + h : 8 * k + h + 1, :] = row[:, at]
            out[:, owner, :, g * d :] = stats[...].T.reshape(n, t // n, 128).astype(BF)

    return pl.pallas_call(
        kernel,
        out_shape=jax.ShapeDtypeStruct((n, n, t // n, width + 128), BF),
        in_specs=[SM] + [VM] * (n + 2 * ns + 4),
        out_specs=VM,
        scratch_shapes=[
            pltpu.VMEM((rows, d), BF),
            pltpu.VMEM((1, rows), F32),
            pltpu.VMEM((1, rows), F32),
            pltpu.VMEM((d, rows), F32),
            pltpu.VMEM((KEYS, rows), F32),
            pltpu.VMEM((KEYS, rows), F32),
            pltpu.VMEM((1, rows), jnp.int32),
            pltpu.VMEM((128, t), F32),
            pltpu.VMEM((room, d), BF),
            pltpu.VMEM((room, d), BF),
        ],
        compiler_params=params(),
        name="attend",
    )(where, *chunks, *keys, *values, *new_pairs[0], *new_pairs[1])


def merge(parts, d):
    n, t, width = parts.shape
    g = (width - 128) // d

    def kernel(ins, out):
        stats = [ins[i, :, g * d :].astype(F32) for i in range(n)]
        for h in range(g):
            tops = [s[:, h : h + 1] + s[:, 8 + h : 9 + h] for s in stats]
            dens = [s[:, 16 + h : 17 + h] + s[:, 24 + h : 25 + h] for s in stats]
            top = functools.reduce(jnp.maximum, tops)
            shares = [jnp.exp(a - top) for a in tops]
            den = sum(w * a for w, a in zip(shares, dens))
            num = sum(w * ins[i, :, h * d : (h + 1) * d].astype(F32) for i, w in enumerate(shares))
            out[:, h * d : (h + 1) * d] = (num / den).astype(BF)

    return pl.pallas_call(
        kernel,
        out_shape=jax.ShapeDtypeStruct((t, g * d), BF),
        in_specs=[VM],
        out_specs=VM,
        compiler_params=params(),
        name="merge",
    )(parts)


def project_out(where, contexts, weights, n):
    t, inner = contexts[0].shape
    cols = weights.shape[0]
    part = t // n

    def kernel(where_ref, *refs):
        c_refs, (w_ref, out, tokens) = refs[:4], refs[4:]
        here = 2 * where_ref[1] + where_ref[2]
        for f in range(4):
            tokens[:, f ^ here] = c_refs[f][...].reshape(n, part, inner).astype(F32)
        rows = tokens[...].reshape(4 * t, inner).astype(BF)
        out[...] = nt(rows, w_ref[...]).astype(BF).reshape(n, 4 * part, cols)

    return pl.pallas_call(
        kernel,
        out_shape=jax.ShapeDtypeStruct((n, 4 * part, cols), BF),
        in_specs=[SM] + [VM] * 5,
        out_specs=VM,
        scratch_shapes=[pltpu.VMEM((n, 4, part, inner), F32)],
        compiler_params=params(),
        name="project_out",
    )(where, *contexts, weights)


def sum_heads(parts, n):
    heads, rows, cols = parts.shape
    width = cols // n

    def kernel(p_ref, out):
        total = p_ref[0].astype(F32)
        for i in range(1, heads):
            total = total + p_ref[i].astype(F32)
        for k in range(n):
            out[k] = total[:, k * width : (k + 1) * width].astype(BF)

    return pl.pallas_call(
        kernel,
        out_shape=jax.ShapeDtypeStruct((n, rows, width), BF),
        in_specs=[VM],
        out_specs=VM,
        compiler_params=params(),
        name="sum_heads",
    )(parts)


def per_device(
    hidden,
    norm_gain,
    w_query,
    key_projection_weight,
    value_projection_weight,
    w_out,
    cache_keys,
    earlier_values,
    cache_len,
    stretch_start,
):
    t, model = hidden.shape
    d = cache_keys.shape[2]
    q_cols = w_query.shape[1]
    kv_cols = key_projection_weight.shape[1]
    nz = lax.axis_size("z")
    z, y, c = lax.axis_index("z"), lax.axis_index("y"), lax.axis_index("c")
    where = jnp.stack([z, y, c, jnp.int32(nz)]).astype(jnp.int32)

    cut = norm_cut(hidden, norm_gain, nz)
    x = lax.all_to_all(cut, ("y", "c"), 0, 0, tiled=True).reshape(4 * t, model // 4)
    near = with_length(cache_keys[0], cache_len)

    weights = side_by_side([w_query, key_projection_weight, value_projection_weight])
    links = {2: x, 3: shift(near, "y", 1)}
    blocks = ring(weights, "z", links)
    x, beside = links[2], links[3]

    keys = [near, beside, shift(near, "c", 1), shift(beside, "c", 1)]

    keep, send = project(where, x, blocks)
    out_cols, keep = lax.optimization_barrier((w_out.T, keep))
    out_cols = lax.all_gather(out_cols, "z", axis=0, tiled=True)

    q_near, q_away, kv = sum_cores(where, keep, shift(send, "c", 1), q_cols)
    queries = (q_near + shift(q_away, "y", 1)).astype(BF)
    near, queries = lax.optimization_barrier((earlier_values[0], queries))
    beside = shift(near, "y", 1)
    values = [near, beside, shift(near, "c", 1), shift(beside, "c", 1)]
    fresh = (kv + shift(kv, "y", 1)).astype(BF).reshape(2 * t, 2 * kv_cols)
    other = shift(fresh, "c", 1)
    new_pairs = [(f[:, :kv_cols], f[:, kv_cols:]) for f in (fresh, other)]

    token = lax.axis_index(BLK) * t + jnp.arange(t, dtype=jnp.int32)
    positions = stretch_start[0] + token
    temper = jnp.log(((positions + 1) // 8192).astype(F32) + 1.0) * 0.1 + 1.0
    scaled = (
        lax.optimization_barrier(queries).astype(F32) * (temper * d ** (-0.5))[:, None]
    ).astype(BF)

    chunks = ring(scaled, "z")
    partial = attend(where, chunks, list(range(nz)), keys, values, new_pairs)
    returned = lax.all_to_all(partial, "z", 0, 0, tiled=True)
    context = merge(returned.reshape(nz, t, -1), d)
    context_y = shift(context, "y", 1)
    contexts = [context, shift(context, "c", 1), context_y, shift(context_y, "c", 1)]
    terms = project_out(where, contexts, out_cols, nz)
    shares = lax.all_to_all(terms, "head", 0, 0, tiled=True)
    final = lax.all_to_all(sum_heads(shares, nz), "z", 0, 0, tiled=True)
    final = final.reshape(nz, 4, t // nz, -1).transpose(1, 0, 2, 3)
    return final.reshape(4 * t, -1)


def solution(mesh):
    finer = Mesh(mesh.devices.reshape(8, 2, 2, mesh.shape["head"]), ("z", "y", "c", "head"))
    return jax.shard_map(
        per_device,
        mesh=finer,
        in_specs=(
            P(BLK, None),
            P(),
            P(BLK, "head"),
            P(BLK, "head"),
            P(BLK, "head"),
            P("head", BLK),
            P("head", BLK, None),
            P("head", BLK, None),
            P(BLK),
            P(),
        ),
        out_specs=P("head", BLK),
        check_vma=False,
    )
```

```python
import functools

import jax
import jax.numpy as jnp
from jax import lax
from jax.experimental import pallas as pl
from jax.experimental.pallas import tpu as pltpu
from jax.sharding import Mesh
from jax.sharding import PartitionSpec as P

BLK = ("z", "y", "c")
BF = jnp.bfloat16
F32 = jnp.float32
NEG = -1e30
KEYS = 512
SPAN = 256


def shift(x, axis, d):
    n = lax.axis_size(axis)
    return lax.ppermute(x, axis, [(i, (i + d) % n) for i in range(n)])


def ring(x, axis, beside=None):
    n = lax.axis_size(axis)
    ahead, behind = [x], [x]
    for step in range(n // 2):
        if beside and step in beside:
            ahead[-1], beside[step] = lax.optimization_barrier((ahead[-1], beside[step]))
        ahead.append(shift(ahead[-1], axis, 1))
        if step < (n - 1) // 2:
            behind.append(shift(behind[-1], axis, -1))
        if beside and step == 0:
            ahead[-1], behind[-1] = lax.optimization_barrier((ahead[-1], behind[-1]))
    return ahead + behind[:0:-1]


def nt(a, b):
    return lax.dot_general(a, b, (((1,), (1,)), ((), ())), preferred_element_type=F32)


def tn(a, b):
    return lax.dot_general(a, b, (((0,), (0,)), ((), ())), preferred_element_type=F32)


VM = pl.BlockSpec(memory_space=pltpu.VMEM)
SM = pl.BlockSpec(memory_space=pltpu.SMEM)


def params(mib=56):
    return pltpu.CompilerParams(vmem_limit_bytes=mib << 20)


def side_by_side(arrays):
    rows = arrays[0].shape[0]
    widths = [a.shape[1] for a in arrays]

    def body(*refs):
        out, at = refs[-1], 0
        for ref, width in zip(refs[:-1], widths):
            out[:, at : at + width] = ref[...]
            at += width

    return pl.pallas_call(
        body,
        out_shape=jax.ShapeDtypeStruct((rows, sum(widths)), arrays[0].dtype),
        in_specs=[VM] * len(arrays),
        out_specs=VM,
        compiler_params=params(),
        name="side_by_side",
    )(*arrays)


def project(where, x, blocks):
    rows, _ = x.shape
    n = len(blocks)
    r, cols = blocks[0].shape
    t = rows // 4

    def kernel(where_ref, x_ref, *refs):
        w_refs, (keep, send, whole, total) = refs[:n], refs[n:]
        z, c = where_ref[0], where_ref[2]
        for d in range(n):
            at = lax.rem(z + (n - d), n)
            whole[pl.ds(pl.multiple_of(at * r, 16), r), :] = w_refs[d][...]
        total[...] = jnp.dot(x_ref[...], whole[...], preferred_element_type=F32).reshape(4, t, cols)
        for y in range(2):
            keep[y] = total[2 * y + c]
            send[y] = total[2 * y + 1 - c]

    half = jax.ShapeDtypeStruct((2, t, cols), F32)
    return pl.pallas_call(
        kernel,
        out_shape=[half, half],
        in_specs=[SM, VM] + [VM] * n,
        out_specs=[VM, VM],
        scratch_shapes=[pltpu.VMEM((n * r, cols), BF), pltpu.VMEM((4, t, cols), F32)],
        compiler_params=params(),
        name="project",
    )(where, x, *blocks)


def sum_cores(where, kept, came, q_cols):
    _, t, cols = kept.shape

    def kernel(where_ref, a_ref, b_ref, near, away, rest):
        y = where_ref[1]
        near[...] = a_ref[y, :, :q_cols] + b_ref[y, :, :q_cols]
        away[...] = a_ref[1 - y, :, :q_cols] + b_ref[1 - y, :, :q_cols]
        rest[...] = a_ref[:, :, q_cols:] + b_ref[:, :, q_cols:]

    q = jax.ShapeDtypeStruct((t, q_cols), F32)
    return pl.pallas_call(
        kernel,
        out_shape=[q, q, jax.ShapeDtypeStruct((2, t, cols - q_cols), F32)],
        in_specs=[SM, VM, VM],
        out_specs=[VM, VM, VM],
        compiler_params=params(),
        name="sum_cores",
    )(where, kept, came)


def norm_cut(hidden, gain, n):
    t, model = hidden.shape
    width = model // (4 * n)

    def kernel(h_ref, g_ref, out):
        x = h_ref[...].astype(F32)
        normed = (
            x * lax.rsqrt(jnp.mean(x * x, axis=-1, keepdims=True) + 1e-05) * g_ref[...]
        ).astype(BF)
        for k in range(n):
            for j in range(4):
                at = (4 * k + j) * width
                out[j, :, k * width : (k + 1) * width] = normed[:, at : at + width]

    return pl.pallas_call(
        kernel,
        out_shape=jax.ShapeDtypeStruct((4, t, n * width), BF),
        in_specs=[VM, VM],
        out_specs=VM,
        compiler_params=params(),
        name="norm_cut",
    )(hidden, gain.reshape(1, model))


TAIL = 16


def with_length(keys, length):
    rows, d = keys.shape

    def kernel(len_ref, k_ref, out):
        out[0:rows, :] = k_ref[...]
        lane = lax.broadcasted_iota(jnp.int32, (TAIL, d), 1)
        digits = jnp.where(lane == 0, len_ref[0] // 64, lax.rem(len_ref[0], 64))
        out[rows:, :] = digits.astype(F32).astype(BF)

    return pl.pallas_call(
        kernel,
        out_shape=jax.ShapeDtypeStruct((rows + TAIL, d), keys.dtype),
        in_specs=[SM, VM],
        out_specs=VM,
        compiler_params=params(),
        name="with_length",
    )(length, keys)


def attend(where, chunks, dists, keys, values, new_pairs):
    n = len(chunks)
    t, width = chunks[0].shape
    each, d = values[0].shape
    ns = len(keys)
    room = ns * each + 2 * KEYS
    g = width // d
    rows = n * g * t
    fresh = new_pairs[0][0].shape[0]

    def kernel(where_ref, *refs):
        q_refs = refs[:n]
        k_in, v_in, refs = refs[n : n + ns], refs[n + ns : n + 2 * ns], refs[n + 2 * ns :]
        nk0, nv0, nk1, nv1 = refs[:4]
        out, q_all, m, l, acc, s_a, s_b, token, stats, k_ref, v_ref = refs[4:]
        top_key = k_in[0][0:1, :]
        at = jnp.int32(0)
        counted = jnp.int32(0)
        lane = lax.broadcasted_iota(jnp.int32, (TAIL, d), 1)
        row = lax.broadcasted_iota(jnp.int32, (TAIL, d), 0)
        place = jnp.where(row > 0, 0.0, jnp.where(lane == 0, 64.0, jnp.where(lane == 1, 1.0, 0.0)))
        for i in range(ns):
            digits = k_in[i][each : each + TAIL, :].astype(F32)
            length = jnp.sum(digits * place).astype(jnp.int32)
            counted = counted + length
            at = pl.multiple_of(at, 16)
            k_ref[pl.ds(at, each), :] = k_in[i][0:each, :]
            v_ref[pl.ds(at, each), :] = v_in[i][...]
            whole = length // 16
            odd = length - whole * 16
            tail = pl.multiple_of(at + whole * 16, 16)

            @pl.when(odd > 0)
            def _():
                valid = lax.broadcasted_iota(jnp.int32, (16, d), 0) < odd
                k_tile = k_ref[pl.ds(tail, 16), :].astype(F32)
                v_tile = v_ref[pl.ds(tail, 16), :].astype(F32)
                k_ref[pl.ds(tail, 16), :] = jnp.where(valid, k_tile, top_key.astype(F32)).astype(BF)
                v_ref[pl.ds(tail, 16), :] = jnp.where(valid, v_tile, 0.0).astype(BF)

            at = at + ((length + 15) // 16) * 16
        used = pl.multiple_of(at, 16)
        k_ref[pl.ds(used, KEYS), :] = jnp.broadcast_to(top_key, (KEYS, d))
        v_ref[pl.ds(used, KEYS), :] = jnp.zeros((KEYS, d), BF)
        z, y, c = where_ref[0], where_ref[1], where_ref[2]
        nz = where_ref[3]
        for i in range(n):
            base = lax.rem(z + nz - dists[i], nz) * (4 * t) + (2 * y + c) * t
            for h in range(g):
                at = (i * g + h) * t
                q_all[at : at + t, :] = q_refs[i][:, h * d : (h + 1) * d]
            span = slice(i * g * t, (i + 1) * g * t)
            token[:, span] = base + lax.rem(lax.broadcasted_iota(jnp.int32, (1, g * t), 1), t)
        m[...] = jnp.full(m.shape, NEG, F32)
        l[...] = jnp.zeros(l.shape, F32)
        acc[...] = jnp.zeros(acc.shape, F32)

        def absorb(s, values, cs):
            before = m[:, cs]
            now = jnp.maximum(before, jnp.max(s, axis=0, keepdims=True))
            fade = jnp.exp(before - now)
            p = jnp.exp(s - now)
            l[:, cs] = l[:, cs] * fade + jnp.sum(p, axis=0, keepdims=True)
            m[:, cs] = now
            acc[:, cs] = acc[:, cs] * fade + tn(values, p.astype(BF))

        def block(ref, u):
            return ref[pl.ds(pl.multiple_of(u * KEYS, KEYS), KEYS), :]

        spans = [slice(lo, lo + SPAN) for lo in range(0, rows, SPAN)]
        blocks = (used + KEYS - 1) // KEYS
        for cs in spans:
            s_a[:, cs] = nt(block(k_ref, 0), q_all[cs, :])

        def visit(u, _):
            for now, then, at in ((s_a, s_b, 2 * u), (s_b, s_a, 2 * u + 1)):
                k_next, v_here = block(k_ref, at + 1), block(v_ref, at)
                for cs in spans:
                    then[:, cs] = nt(k_next, q_all[cs, :])
                    absorb(now[:, cs], v_here, cs)
            return 0

        lax.fori_loop(0, blocks // 2, visit, 0)

        @pl.when(lax.rem(blocks, 2) == 1)
        def _():
            v_last = block(v_ref, blocks - 1)
            for cs in spans:
                absorb(s_a[:, cs], v_last, cs)

        extra = (blocks * KEYS - counted).astype(F32)
        first = nt(k_ref[0:8, :], q_all[...])[0:1]
        l[...] = l[...] - extra * jnp.exp(first - m[...])
        for part, (nk, nv) in enumerate(((nk0, nv0), (nk1, nv1))):
            row = lax.broadcasted_iota(jnp.int32, (fresh, 1), 0)
            side = c if part == 0 else 1 - c
            key_token = z * (4 * t) + (row // t) * (2 * t) + side * t + lax.rem(row, t)
            for cs in spans:
                s = nt(nk[...], q_all[cs, :])
                absorb(jnp.where(key_token <= token[:, cs], s, NEG), nv[...], cs)
        top = m[...]
        top_hi = top.astype(BF).astype(F32)
        top_lo = (top - top_hi).astype(BF).astype(F32)
        scale = jnp.exp(top - (top_hi + top_lo))
        den = l[...] * scale
        den_hi = den.astype(BF).astype(F32)
        den_lo = den - den_hi
        numer = (acc[...] * scale).T
        stats[...] = jnp.zeros(stats.shape, F32)
        for i in range(n):
            owner = lax.rem(z + nz - dists[i], nz)
            for h in range(g):
                at = slice((i * g + h) * t, (i * g + h + 1) * t)
                out[:, owner, :, h * d : (h + 1) * d] = numer[at].reshape(n, t // n, d).astype(BF)
                for k, row in enumerate((top_hi, top_lo, den_hi, den_lo)):
                    stats[8 * k + h : 8 * k + h + 1, :] = row[:, at]
            out[:, owner, :, g * d :] = stats[...].T.reshape(n, t // n, 128).astype(BF)

    return pl.pallas_call(
        kernel,
        out_shape=jax.ShapeDtypeStruct((n, n, t // n, width + 128), BF),
        in_specs=[SM] + [VM] * (n + 2 * ns + 4),
        out_specs=VM,
        scratch_shapes=[
            pltpu.VMEM((rows, d), BF),
            pltpu.VMEM((1, rows), F32),
            pltpu.VMEM((1, rows), F32),
            pltpu.VMEM((d, rows), F32),
            pltpu.VMEM((KEYS, rows), F32),
            pltpu.VMEM((KEYS, rows), F32),
            pltpu.VMEM((1, rows), jnp.int32),
            pltpu.VMEM((128, t), F32),
            pltpu.VMEM((room, d), BF),
            pltpu.VMEM((room, d), BF),
        ],
        compiler_params=params(),
        name="attend",
    )(where, *chunks, *keys, *values, *new_pairs[0], *new_pairs[1])


def merge(parts, d):
    n, t, width = parts.shape
    g = (width - 128) // d

    def kernel(ins, out):
        stats = [ins[i, :, g * d :].astype(F32) for i in range(n)]
        for h in range(g):
            tops = [s[:, h : h + 1] + s[:, 8 + h : 9 + h] for s in stats]
            dens = [s[:, 16 + h : 17 + h] + s[:, 24 + h : 25 + h] for s in stats]
            top = functools.reduce(jnp.maximum, tops)
            shares = [jnp.exp(a - top) for a in tops]
            den = sum(w * a for w, a in zip(shares, dens))
            num = sum(w * ins[i, :, h * d : (h + 1) * d].astype(F32) for i, w in enumerate(shares))
            out[:, h * d : (h + 1) * d] = (num / den).astype(BF)

    return pl.pallas_call(
        kernel,
        out_shape=jax.ShapeDtypeStruct((t, g * d), BF),
        in_specs=[VM],
        out_specs=VM,
        compiler_params=params(),
        name="merge",
    )(parts)


def project_out(where, contexts, weights, n):
    t, inner = contexts[0].shape
    cols = weights.shape[0]
    part = t // n

    def kernel(where_ref, *refs):
        c_refs, (w_ref, out, tokens) = refs[:4], refs[4:]
        here = 2 * where_ref[1] + where_ref[2]
        for f in range(4):
            tokens[:, f ^ here] = c_refs[f][...].reshape(n, part, inner).astype(F32)
        rows = tokens[...].reshape(4 * t, inner).astype(BF)
        out[...] = nt(rows, w_ref[...]).astype(BF).reshape(n, 4 * part, cols)

    return pl.pallas_call(
        kernel,
        out_shape=jax.ShapeDtypeStruct((n, 4 * part, cols), BF),
        in_specs=[SM] + [VM] * 5,
        out_specs=VM,
        scratch_shapes=[pltpu.VMEM((n, 4, part, inner), F32)],
        compiler_params=params(),
        name="project_out",
    )(where, *contexts, weights)


def sum_heads(parts, n):
    heads, rows, cols = parts.shape
    width = cols // n

    def kernel(p_ref, out):
        total = p_ref[0].astype(F32)
        for i in range(1, heads):
            total = total + p_ref[i].astype(F32)
        for k in range(n):
            out[k] = total[:, k * width : (k + 1) * width].astype(BF)

    return pl.pallas_call(
        kernel,
        out_shape=jax.ShapeDtypeStruct((n, rows, width), BF),
        in_specs=[VM],
        out_specs=VM,
        compiler_params=params(),
        name="sum_heads",
    )(parts)


def per_device(
    hidden,
    norm_gain,
    w_query,
    key_projection_weight,
    value_projection_weight,
    w_out,
    cache_keys,
    earlier_values,
    cache_len,
    stretch_start,
):
    t, model = hidden.shape
    d = cache_keys.shape[2]
    q_cols = w_query.shape[1]
    kv_cols = key_projection_weight.shape[1]
    nz = lax.axis_size("z")
    z, y, c = lax.axis_index("z"), lax.axis_index("y"), lax.axis_index("c")
    where = jnp.stack([z, y, c, jnp.int32(nz)]).astype(jnp.int32)

    cut = norm_cut(hidden, norm_gain, nz)
    x = lax.all_to_all(cut, ("y", "c"), 0, 0, tiled=True).reshape(4 * t, model // 4)
    near = with_length(cache_keys[0], cache_len)

    weights = side_by_side([w_query, key_projection_weight, value_projection_weight])
    links = {2: shift(near, "y", 1), 3: x}
    blocks = ring(weights, "z", links)
    beside, x = links[2], links[3]

    keys = [near, beside, shift(near, "c", 1), shift(beside, "c", 1)]

    keep, send = project(where, x, blocks)
    out_cols, keep = lax.optimization_barrier((w_out.T, keep))
    out_cols = lax.all_gather(out_cols, "z", axis=0, tiled=True)

    near, _ = lax.optimization_barrier((earlier_values[0], x))
    beside, came = lax.optimization_barrier((shift(near, "y", 1), shift(send, "c", 1)))
    values = [near, beside, shift(near, "c", 1), shift(beside, "c", 1)]
    q_near, q_away, kv = sum_cores(where, keep, came, q_cols)
    queries = (q_near + shift(q_away, "y", 1)).astype(BF)
    fresh = (kv + shift(kv, "y", 1)).astype(BF).reshape(2 * t, 2 * kv_cols)
    other = shift(fresh, "c", 1)
    new_pairs = [(f[:, :kv_cols], f[:, kv_cols:]) for f in (fresh, other)]

    token = lax.axis_index(BLK) * t + jnp.arange(t, dtype=jnp.int32)
    positions = stretch_start[0] + token
    temper = jnp.log(((positions + 1) // 8192).astype(F32) + 1.0) * 0.1 + 1.0
    scaled = (
        lax.optimization_barrier(queries).astype(F32) * (temper * d ** (-0.5))[:, None]
    ).astype(BF)

    chunks = ring(scaled, "z")
    partial = attend(where, chunks, list(range(nz)), keys, values, new_pairs)
    returned = lax.all_to_all(partial, "z", 0, 0, tiled=True)
    context = merge(returned.reshape(nz, t, -1), d)
    context_y = shift(context, "y", 1)
    contexts = [context, shift(context, "c", 1), context_y, shift(context_y, "c", 1)]
    terms = project_out(where, contexts, out_cols, nz)
    shares = lax.all_to_all(terms, "head", 0, 0, tiled=True)
    final = lax.all_to_all(sum_heads(shares, nz), "z", 0, 0, tiled=True)
    final = final.reshape(nz, 4, t // nz, -1).transpose(1, 0, 2, 3)
    return final.reshape(4 * t, -1)


def solution(mesh):
    finer = Mesh(mesh.devices.reshape(8, 2, 2, mesh.shape["head"]), ("z", "y", "c", "head"))
    return jax.shard_map(
        per_device,
        mesh=finer,
        in_specs=(
            P(BLK, None),
            P(),
            P(BLK, "head"),
            P(BLK, "head"),
            P(BLK, "head"),
            P("head", BLK),
            P("head", BLK, None),
            P("head", BLK, None),
            P(BLK),
            P(),
        ),
        out_specs=P("head", BLK),
        check_vma=False,
    )
```

```python
import functools

import jax
import jax.numpy as jnp
from jax import lax
from jax.experimental import pallas as pl
from jax.experimental.pallas import tpu as pltpu
from jax.sharding import Mesh
from jax.sharding import PartitionSpec as P

BLK = ("z", "y", "c")
BF = jnp.bfloat16
F32 = jnp.float32
NEG = -1e30
KEYS = 512
SPAN = 256


def shift(x, axis, d):
    n = lax.axis_size(axis)
    return lax.ppermute(x, axis, [(i, (i + d) % n) for i in range(n)])


def ring(x, axis, beside=None):
    n = lax.axis_size(axis)
    ahead, behind = [x], [x]
    for step in range(n // 2):
        if beside and step in beside:
            ahead[-1], beside[step] = lax.optimization_barrier((ahead[-1], beside[step]))
        ahead.append(shift(ahead[-1], axis, 1))
        if step < (n - 1) // 2:
            behind.append(shift(behind[-1], axis, -1))
        if beside and step < (n - 1) // 2:
            ahead[-1], behind[-1] = lax.optimization_barrier((ahead[-1], behind[-1]))
    return ahead + behind[:0:-1]


def nt(a, b):
    return lax.dot_general(a, b, (((1,), (1,)), ((), ())), preferred_element_type=F32)


def tn(a, b):
    return lax.dot_general(a, b, (((0,), (0,)), ((), ())), preferred_element_type=F32)


VM = pl.BlockSpec(memory_space=pltpu.VMEM)
SM = pl.BlockSpec(memory_space=pltpu.SMEM)


def params(mib=56):
    return pltpu.CompilerParams(vmem_limit_bytes=mib << 20)


def side_by_side(arrays):
    rows = arrays[0].shape[0]
    widths = [a.shape[1] for a in arrays]

    def body(*refs):
        out, at = refs[-1], 0
        for ref, width in zip(refs[:-1], widths):
            out[:, at : at + width] = ref[...]
            at += width

    return pl.pallas_call(
        body,
        out_shape=jax.ShapeDtypeStruct((rows, sum(widths)), arrays[0].dtype),
        in_specs=[VM] * len(arrays),
        out_specs=VM,
        compiler_params=params(),
        name="side_by_side",
    )(*arrays)


def project(where, x, blocks):
    rows, _ = x.shape
    n = len(blocks)
    r, cols = blocks[0].shape
    t = rows // 4

    def kernel(where_ref, x_ref, *refs):
        w_refs, (keep, send, whole, total) = refs[:n], refs[n:]
        z, c = where_ref[0], where_ref[2]
        for d in range(n):
            at = lax.rem(z + (n - d), n)
            whole[pl.ds(pl.multiple_of(at * r, 16), r), :] = w_refs[d][...]
        total[...] = jnp.dot(x_ref[...], whole[...], preferred_element_type=F32).reshape(4, t, cols)
        for y in range(2):
            keep[y] = total[2 * y + c]
            send[y] = total[2 * y + 1 - c]

    half = jax.ShapeDtypeStruct((2, t, cols), F32)
    return pl.pallas_call(
        kernel,
        out_shape=[half, half],
        in_specs=[SM, VM] + [VM] * n,
        out_specs=[VM, VM],
        scratch_shapes=[pltpu.VMEM((n * r, cols), BF), pltpu.VMEM((4, t, cols), F32)],
        compiler_params=params(),
        name="project",
    )(where, x, *blocks)


def sum_cores(where, kept, came, q_cols):
    _, t, cols = kept.shape

    def kernel(where_ref, a_ref, b_ref, near, away, rest):
        y = where_ref[1]
        near[...] = a_ref[y, :, :q_cols] + b_ref[y, :, :q_cols]
        away[...] = a_ref[1 - y, :, :q_cols] + b_ref[1 - y, :, :q_cols]
        rest[...] = a_ref[:, :, q_cols:] + b_ref[:, :, q_cols:]

    q = jax.ShapeDtypeStruct((t, q_cols), F32)
    return pl.pallas_call(
        kernel,
        out_shape=[q, q, jax.ShapeDtypeStruct((2, t, cols - q_cols), F32)],
        in_specs=[SM, VM, VM],
        out_specs=[VM, VM, VM],
        compiler_params=params(),
        name="sum_cores",
    )(where, kept, came)


def norm_cut(hidden, gain, n):
    t, model = hidden.shape
    width = model // (4 * n)

    def kernel(h_ref, g_ref, out):
        x = h_ref[...].astype(F32)
        normed = (
            x * lax.rsqrt(jnp.mean(x * x, axis=-1, keepdims=True) + 1e-05) * g_ref[...]
        ).astype(BF)
        for k in range(n):
            for j in range(4):
                at = (4 * k + j) * width
                out[j, :, k * width : (k + 1) * width] = normed[:, at : at + width]

    return pl.pallas_call(
        kernel,
        out_shape=jax.ShapeDtypeStruct((4, t, n * width), BF),
        in_specs=[VM, VM],
        out_specs=VM,
        compiler_params=params(),
        name="norm_cut",
    )(hidden, gain.reshape(1, model))


TAIL = 16


def with_length(keys, length):
    rows, d = keys.shape

    def kernel(len_ref, k_ref, out):
        out[0:rows, :] = k_ref[...]
        lane = lax.broadcasted_iota(jnp.int32, (TAIL, d), 1)
        digits = jnp.where(lane == 0, len_ref[0] // 64, lax.rem(len_ref[0], 64))
        out[rows:, :] = digits.astype(F32).astype(BF)

    return pl.pallas_call(
        kernel,
        out_shape=jax.ShapeDtypeStruct((rows + TAIL, d), keys.dtype),
        in_specs=[SM, VM],
        out_specs=VM,
        compiler_params=params(),
        name="with_length",
    )(length, keys)


def attend(where, chunks, dists, keys, values, fresh_pair):
    n = len(chunks)
    t, width = chunks[0].shape
    each, d = values[0].shape
    ns = len(keys)
    room = ns * each + 2 * KEYS
    g = width // d
    rows = n * g * t
    fresh = fresh_pair[0].shape[0]

    def kernel(where_ref, *refs):
        q_refs = refs[:n]
        k_in, v_in, refs = refs[n : n + ns], refs[n + ns : n + 2 * ns], refs[n + 2 * ns :]
        fresh_refs = refs[:2]
        out, q_all, m, l, acc, s_a, s_b, token, stats, k_ref, v_ref = refs[2:]
        top_key = k_in[0][0:1, :]
        at = jnp.int32(0)
        counted = jnp.int32(0)
        lane = lax.broadcasted_iota(jnp.int32, (TAIL, d), 1)
        row = lax.broadcasted_iota(jnp.int32, (TAIL, d), 0)
        place = jnp.where(row > 0, 0.0, jnp.where(lane == 0, 64.0, jnp.where(lane == 1, 1.0, 0.0)))
        for i in range(ns):
            digits = k_in[i][each : each + TAIL, :].astype(F32)
            length = jnp.sum(digits * place).astype(jnp.int32)
            counted = counted + length
            at = pl.multiple_of(at, 16)
            k_ref[pl.ds(at, each), :] = k_in[i][0:each, :]
            v_ref[pl.ds(at, each), :] = v_in[i][...]
            whole = length // 16
            odd = length - whole * 16
            tail = pl.multiple_of(at + whole * 16, 16)

            @pl.when(odd > 0)
            def _():
                valid = lax.broadcasted_iota(jnp.int32, (16, d), 0) < odd
                k_tile = k_ref[pl.ds(tail, 16), :].astype(F32)
                v_tile = v_ref[pl.ds(tail, 16), :].astype(F32)
                k_ref[pl.ds(tail, 16), :] = jnp.where(valid, k_tile, top_key.astype(F32)).astype(BF)
                v_ref[pl.ds(tail, 16), :] = jnp.where(valid, v_tile, 0.0).astype(BF)

            at = at + ((length + 15) // 16) * 16
        used = pl.multiple_of(at, 16)
        k_ref[pl.ds(used, KEYS), :] = jnp.broadcast_to(top_key, (KEYS, d))
        v_ref[pl.ds(used, KEYS), :] = jnp.zeros((KEYS, d), BF)
        z, y, c = where_ref[0], where_ref[1], where_ref[2]
        nz = where_ref[3]
        for i in range(n):
            base = lax.rem(z + nz - dists[i], nz) * (4 * t) + (2 * y + c) * t
            for h in range(g):
                at = (i * g + h) * t
                q_all[at : at + t, :] = q_refs[i][:, h * d : (h + 1) * d]
            span = slice(i * g * t, (i + 1) * g * t)
            token[:, span] = base + lax.rem(lax.broadcasted_iota(jnp.int32, (1, g * t), 1), t)
        m[...] = jnp.full(m.shape, NEG, F32)
        l[...] = jnp.zeros(l.shape, F32)
        acc[...] = jnp.zeros(acc.shape, F32)

        def absorb(s, values, cs):
            before = m[:, cs]
            now = jnp.maximum(before, jnp.max(s, axis=0, keepdims=True))
            fade = jnp.exp(before - now)
            p = jnp.exp(s - now)
            l[:, cs] = l[:, cs] * fade + jnp.sum(p, axis=0, keepdims=True)
            m[:, cs] = now
            acc[:, cs] = acc[:, cs] * fade + tn(values, p.astype(BF))

        def block(ref, u):
            return ref[pl.ds(pl.multiple_of(u * KEYS, KEYS), KEYS), :]

        spans = [slice(lo, lo + SPAN) for lo in range(0, rows, SPAN)]
        blocks = (used + KEYS - 1) // KEYS
        for cs in spans:
            s_a[:, cs] = nt(block(k_ref, 0), q_all[cs, :])

        def visit(u, _):
            for now, then, at in ((s_a, s_b, 2 * u), (s_b, s_a, 2 * u + 1)):
                k_next, v_here = block(k_ref, at + 1), block(v_ref, at)
                for cs in spans:
                    then[:, cs] = nt(k_next, q_all[cs, :])
                    absorb(now[:, cs], v_here, cs)
            return 0

        lax.fori_loop(0, blocks // 2, visit, 0)

        @pl.when(lax.rem(blocks, 2) == 1)
        def _():
            v_last = block(v_ref, blocks - 1)
            for cs in spans:
                absorb(s_a[:, cs], v_last, cs)

        extra = (blocks * KEYS - counted).astype(F32)
        first = nt(k_ref[0:8, :], q_all[...])[0:1]
        l[...] = l[...] - extra * jnp.exp(first - m[...])
        for part, kv_ref in enumerate(fresh_refs):
            new_keys, new_values = kv_ref[:, :d], kv_ref[:, d:]
            row = lax.broadcasted_iota(jnp.int32, (fresh, 1), 0)
            side = c if part == 0 else 1 - c
            key_token = z * (4 * t) + (row // t) * (2 * t) + side * t + lax.rem(row, t)
            for cs in spans:
                s = nt(new_keys, q_all[cs, :])
                absorb(jnp.where(key_token <= token[:, cs], s, NEG), new_values, cs)
        top = m[...]
        top_hi = top.astype(BF).astype(F32)
        top_lo = (top - top_hi).astype(BF).astype(F32)
        scale = jnp.exp(top - (top_hi + top_lo))
        den = l[...] * scale
        den_hi = den.astype(BF).astype(F32)
        den_lo = den - den_hi
        numer = (acc[...] * scale).T
        stats[...] = jnp.zeros(stats.shape, F32)
        for i in range(n):
            owner = lax.rem(z + nz - dists[i], nz)
            for h in range(g):
                at = slice((i * g + h) * t, (i * g + h + 1) * t)
                out[:, owner, :, h * d : (h + 1) * d] = numer[at].reshape(n, t // n, d).astype(BF)
                for k, row in enumerate((top_hi, top_lo, den_hi, den_lo)):
                    stats[8 * k + h : 8 * k + h + 1, :] = row[:, at]
            out[:, owner, :, g * d :] = stats[...].T.reshape(n, t // n, 128).astype(BF)

    return pl.pallas_call(
        kernel,
        out_shape=jax.ShapeDtypeStruct((n, n, t // n, width + 128), BF),
        in_specs=[SM] + [VM] * (n + 2 * ns + 2),
        out_specs=VM,
        scratch_shapes=[
            pltpu.VMEM((rows, d), BF),
            pltpu.VMEM((1, rows), F32),
            pltpu.VMEM((1, rows), F32),
            pltpu.VMEM((d, rows), F32),
            pltpu.VMEM((KEYS, rows), F32),
            pltpu.VMEM((KEYS, rows), F32),
            pltpu.VMEM((1, rows), jnp.int32),
            pltpu.VMEM((128, t), F32),
            pltpu.VMEM((room, d), BF),
            pltpu.VMEM((room, d), BF),
        ],
        compiler_params=params(),
        name="attend",
    )(where, *chunks, *keys, *values, *fresh_pair)


def merge(parts, d):
    n, t, width = parts.shape
    g = (width - 128) // d

    def kernel(ins, out):
        stats = [ins[i, :, g * d :].astype(F32) for i in range(n)]
        for h in range(g):
            tops = [s[:, h : h + 1] + s[:, 8 + h : 9 + h] for s in stats]
            dens = [s[:, 16 + h : 17 + h] + s[:, 24 + h : 25 + h] for s in stats]
            top = functools.reduce(jnp.maximum, tops)
            shares = [jnp.exp(a - top) for a in tops]
            den = sum(w * a for w, a in zip(shares, dens))
            num = sum(w * ins[i, :, h * d : (h + 1) * d].astype(F32) for i, w in enumerate(shares))
            out[:, h * d : (h + 1) * d] = (num / den).astype(BF)

    return pl.pallas_call(
        kernel,
        out_shape=jax.ShapeDtypeStruct((t, g * d), BF),
        in_specs=[VM],
        out_specs=VM,
        compiler_params=params(),
        name="merge",
    )(parts)


def project_out(where, contexts, weights, n):
    t, inner = contexts[0].shape
    cols = weights.shape[0]
    part = t // n

    def kernel(where_ref, *refs):
        c_refs, (w_ref, out, tokens) = refs[:4], refs[4:]
        here = 2 * where_ref[1] + where_ref[2]
        for f in range(4):
            tokens[:, f ^ here] = c_refs[f][...].reshape(n, part, inner).astype(F32)
        rows = tokens[...].reshape(4 * t, inner).astype(BF)
        out[...] = nt(rows, w_ref[...]).astype(BF).reshape(n, 4 * part, cols)

    return pl.pallas_call(
        kernel,
        out_shape=jax.ShapeDtypeStruct((n, 4 * part, cols), BF),
        in_specs=[SM] + [VM] * 5,
        out_specs=VM,
        scratch_shapes=[pltpu.VMEM((n, 4, part, inner), F32)],
        compiler_params=params(),
        name="project_out",
    )(where, *contexts, weights)


def sum_heads(parts, n):
    heads, rows, cols = parts.shape
    width = cols // n

    def kernel(p_ref, out):
        total = p_ref[0].astype(F32)
        for i in range(1, heads):
            total = total + p_ref[i].astype(F32)
        for k in range(n):
            out[k] = total[:, k * width : (k + 1) * width].astype(BF)

    return pl.pallas_call(
        kernel,
        out_shape=jax.ShapeDtypeStruct((n, rows, width), BF),
        in_specs=[VM],
        out_specs=VM,
        compiler_params=params(),
        name="sum_heads",
    )(parts)


def per_device(
    hidden,
    norm_gain,
    w_query,
    key_projection_weight,
    value_projection_weight,
    w_out,
    cache_keys,
    earlier_values,
    cache_len,
    stretch_start,
):
    t, model = hidden.shape
    d = cache_keys.shape[2]
    q_cols = w_query.shape[1]
    kv_cols = key_projection_weight.shape[1]
    nz = lax.axis_size("z")
    z, y, c = lax.axis_index("z"), lax.axis_index("y"), lax.axis_index("c")
    where = jnp.stack([z, y, c, jnp.int32(nz)]).astype(jnp.int32)

    cut = norm_cut(hidden, norm_gain, nz)
    x = lax.all_to_all(cut, ("y", "c"), 0, 0, tiled=True).reshape(4 * t, model // 4)
    near = with_length(cache_keys[0], cache_len)

    weights = side_by_side([w_query, key_projection_weight, value_projection_weight])
    links = {1: cut, 2: shift(near, "y", 1), 3: x}
    blocks = ring(weights, "z", links)
    beside, x = links[2], links[3]

    keys = [near, beside, shift(near, "c", 1), shift(beside, "c", 1)]

    keep, send = project(where, x, blocks)
    out_cols, keep = lax.optimization_barrier((w_out.T, keep))
    out_cols = lax.all_gather(out_cols, "z", axis=0, tiled=True)

    near, _ = lax.optimization_barrier((earlier_values[0], x))
    beside, came = lax.optimization_barrier((shift(near, "y", 1), shift(send, "c", 1)))
    values = [near, beside, shift(near, "c", 1), shift(beside, "c", 1)]
    q_near, q_away, kv = sum_cores(where, keep, came, q_cols)
    queries = (q_near + shift(q_away, "y", 1)).astype(BF)
    fresh = (kv + shift(kv, "y", 1)).astype(BF).reshape(2 * t, 2 * kv_cols)
    other = shift(fresh, "c", 1)

    token = lax.axis_index(BLK) * t + jnp.arange(t, dtype=jnp.int32)
    positions = stretch_start[0] + token
    temper = jnp.log(((positions + 1) // 8192).astype(F32) + 1.0) * 0.1 + 1.0
    scaled = (
        lax.optimization_barrier(queries).astype(F32) * (temper * d ** (-0.5))[:, None]
    ).astype(BF)

    chunks = ring(scaled, "z")
    partial = attend(where, chunks, list(range(nz)), keys, values, (fresh, other))
    returned = lax.all_to_all(partial, "z", 0, 0, tiled=True)
    context = merge(returned.reshape(nz, t, -1), d)
    context_y = shift(context, "y", 1)
    contexts = [context, shift(context, "c", 1), context_y, shift(context_y, "c", 1)]
    terms = project_out(where, contexts, out_cols, nz)
    shares = lax.all_to_all(terms, "head", 0, 0, tiled=True)
    final = lax.all_to_all(sum_heads(shares, nz), "z", 0, 0, tiled=True)
    final = final.reshape(nz, 4, t // nz, -1).transpose(1, 0, 2, 3)
    return final.reshape(4 * t, -1)


def solution(mesh):
    finer = Mesh(mesh.devices.reshape(8, 2, 2, mesh.shape["head"]), ("z", "y", "c", "head"))
    return jax.shard_map(
        per_device,
        mesh=finer,
        in_specs=(
            P(BLK, None),
            P(),
            P(BLK, "head"),
            P(BLK, "head"),
            P(BLK, "head"),
            P("head", BLK),
            P("head", BLK, None),
            P("head", BLK, None),
            P(BLK),
            P(),
        ),
        out_specs=P("head", BLK),
        check_vma=False,
    )
```

```python
import functools

import jax
import jax.numpy as jnp
from jax import lax
from jax.experimental import pallas as pl
from jax.experimental.pallas import tpu as pltpu
from jax.sharding import Mesh
from jax.sharding import PartitionSpec as P

BLK = ("z", "y", "c")
BF = jnp.bfloat16
F32 = jnp.float32
NEG = -1e30
KEYS = 512
SPAN = 256


def shift(x, axis, d):
    n = lax.axis_size(axis)
    return lax.ppermute(x, axis, [(i, (i + d) % n) for i in range(n)])


def ring(x, axis, beside=None):
    n = lax.axis_size(axis)
    ahead, behind = [x], [x]
    for step in range(n // 2):
        if beside and step in beside:
            ahead[-1], beside[step] = lax.optimization_barrier((ahead[-1], beside[step]))
        ahead.append(shift(ahead[-1], axis, 1))
        if step < (n - 1) // 2:
            behind.append(shift(behind[-1], axis, -1))
        if beside and step < (n - 1) // 2:
            ahead[-1], behind[-1] = lax.optimization_barrier((ahead[-1], behind[-1]))
    return ahead + behind[:0:-1]


def nt(a, b):
    return lax.dot_general(a, b, (((1,), (1,)), ((), ())), preferred_element_type=F32)


def tn(a, b):
    return lax.dot_general(a, b, (((0,), (0,)), ((), ())), preferred_element_type=F32)


VM = pl.BlockSpec(memory_space=pltpu.VMEM)
SM = pl.BlockSpec(memory_space=pltpu.SMEM)


def params(mib=56):
    return pltpu.CompilerParams(vmem_limit_bytes=mib << 20)


def side_by_side(arrays):
    rows = arrays[0].shape[0]
    widths = [a.shape[1] for a in arrays]

    def body(*refs):
        out, at = refs[-1], 0
        for ref, width in zip(refs[:-1], widths):
            out[:, at : at + width] = ref[...]
            at += width

    return pl.pallas_call(
        body,
        out_shape=jax.ShapeDtypeStruct((rows, sum(widths)), arrays[0].dtype),
        in_specs=[VM] * len(arrays),
        out_specs=VM,
        compiler_params=params(),
        name="side_by_side",
    )(*arrays)


def project(where, x, blocks):
    rows, _ = x.shape
    n = len(blocks)
    r, cols = blocks[0].shape
    t = rows // 4

    def kernel(where_ref, x_ref, *refs):
        w_refs, (keep, send, whole, total) = refs[:n], refs[n:]
        z, c = where_ref[0], where_ref[2]
        for d in range(n):
            at = lax.rem(z + (n - d), n)
            whole[pl.ds(pl.multiple_of(at * r, 16), r), :] = w_refs[d][...]
        total[...] = jnp.dot(x_ref[...], whole[...], preferred_element_type=F32).reshape(4, t, cols)
        for y in range(2):
            keep[y] = total[2 * y + c]
            send[y] = total[2 * y + 1 - c]

    half = jax.ShapeDtypeStruct((2, t, cols), F32)
    return pl.pallas_call(
        kernel,
        out_shape=[half, half],
        in_specs=[SM, VM] + [VM] * n,
        out_specs=[VM, VM],
        scratch_shapes=[pltpu.VMEM((n * r, cols), BF), pltpu.VMEM((4, t, cols), F32)],
        compiler_params=params(),
        name="project",
    )(where, x, *blocks)


def sum_cores(where, kept, came, q_cols):
    _, t, cols = kept.shape

    def kernel(where_ref, a_ref, b_ref, near, away, rest):
        y = where_ref[1]
        near[...] = a_ref[y, :, :q_cols] + b_ref[y, :, :q_cols]
        away[...] = a_ref[1 - y, :, :q_cols] + b_ref[1 - y, :, :q_cols]
        rest[...] = a_ref[:, :, q_cols:] + b_ref[:, :, q_cols:]

    q = jax.ShapeDtypeStruct((t, q_cols), F32)
    return pl.pallas_call(
        kernel,
        out_shape=[q, q, jax.ShapeDtypeStruct((2, t, cols - q_cols), F32)],
        in_specs=[SM, VM, VM],
        out_specs=[VM, VM, VM],
        compiler_params=params(),
        name="sum_cores",
    )(where, kept, came)


def norm_cut(hidden, gain, n):
    t, model = hidden.shape
    width = model // (4 * n)

    def kernel(h_ref, g_ref, out):
        x = h_ref[...].astype(F32)
        normed = (
            x * lax.rsqrt(jnp.mean(x * x, axis=-1, keepdims=True) + 1e-05) * g_ref[...]
        ).astype(BF)
        for k in range(n):
            for j in range(4):
                at = (4 * k + j) * width
                out[j, :, k * width : (k + 1) * width] = normed[:, at : at + width]

    return pl.pallas_call(
        kernel,
        out_shape=jax.ShapeDtypeStruct((4, t, n * width), BF),
        in_specs=[VM, VM],
        out_specs=VM,
        compiler_params=params(),
        name="norm_cut",
    )(hidden, gain.reshape(1, model))


TAIL = 16


def with_length(keys, length):
    rows, d = keys.shape

    def kernel(len_ref, k_ref, out):
        out[0:rows, :] = k_ref[...]
        lane = lax.broadcasted_iota(jnp.int32, (TAIL, d), 1)
        digits = jnp.where(lane == 0, len_ref[0] // 64, lax.rem(len_ref[0], 64))
        out[rows:, :] = digits.astype(F32).astype(BF)

    return pl.pallas_call(
        kernel,
        out_shape=jax.ShapeDtypeStruct((rows + TAIL, d), keys.dtype),
        in_specs=[SM, VM],
        out_specs=VM,
        compiler_params=params(),
        name="with_length",
    )(length, keys)


def attend(where, chunks, dists, keys, values, fresh_pair):
    n = len(chunks)
    t, width = chunks[0].shape
    each, d = values[0].shape
    ns = len(keys)
    room = ns * each + 2 * KEYS
    g = width // d
    rows = n * g * t
    fresh = fresh_pair[0].shape[0]

    def kernel(where_ref, *refs):
        q_refs = refs[:n]
        k_in, v_in, refs = refs[n : n + ns], refs[n + ns : n + 2 * ns], refs[n + 2 * ns :]
        fresh_refs = refs[:2]
        out, q_all, m, l, acc, s_a, s_b, token, stats, k_ref, v_ref = refs[2:]
        top_key = k_in[0][0:1, :]
        at = jnp.int32(0)
        counted = jnp.int32(0)
        lane = lax.broadcasted_iota(jnp.int32, (TAIL, d), 1)
        row = lax.broadcasted_iota(jnp.int32, (TAIL, d), 0)
        place = jnp.where(row > 0, 0.0, jnp.where(lane == 0, 64.0, jnp.where(lane == 1, 1.0, 0.0)))
        for i in range(ns):
            digits = k_in[i][each : each + TAIL, :].astype(F32)
            length = jnp.sum(digits * place).astype(jnp.int32)
            counted = counted + length
            at = pl.multiple_of(at, 16)
            k_ref[pl.ds(at, each), :] = k_in[i][0:each, :]
            v_ref[pl.ds(at, each), :] = v_in[i][...]
            whole = length // 16
            odd = length - whole * 16
            tail = pl.multiple_of(at + whole * 16, 16)

            @pl.when(odd > 0)
            def _():
                valid = lax.broadcasted_iota(jnp.int32, (16, d), 0) < odd
                k_tile = k_ref[pl.ds(tail, 16), :].astype(F32)
                v_tile = v_ref[pl.ds(tail, 16), :].astype(F32)
                k_ref[pl.ds(tail, 16), :] = jnp.where(valid, k_tile, top_key.astype(F32)).astype(BF)
                v_ref[pl.ds(tail, 16), :] = jnp.where(valid, v_tile, 0.0).astype(BF)

            at = at + ((length + 15) // 16) * 16
        used = pl.multiple_of(at, 16)
        k_ref[pl.ds(used, KEYS), :] = jnp.broadcast_to(top_key, (KEYS, d))
        v_ref[pl.ds(used, KEYS), :] = jnp.zeros((KEYS, d), BF)
        z, y, c = where_ref[0], where_ref[1], where_ref[2]
        nz = where_ref[3]
        for i in range(n):
            base = lax.rem(z + nz - dists[i], nz) * (4 * t) + (2 * y + c) * t
            for h in range(g):
                at = (i * g + h) * t
                q_all[at : at + t, :] = q_refs[i][:, h * d : (h + 1) * d]
            span = slice(i * g * t, (i + 1) * g * t)
            token[:, span] = base + lax.rem(lax.broadcasted_iota(jnp.int32, (1, g * t), 1), t)
        m[...] = jnp.full(m.shape, NEG, F32)
        l[...] = jnp.zeros(l.shape, F32)
        acc[...] = jnp.zeros(acc.shape, F32)

        def absorb(s, values, cs):
            before = m[:, cs]
            now = jnp.maximum(before, jnp.max(s, axis=0, keepdims=True))
            fade = jnp.exp(before - now)
            p = jnp.exp(s - now)
            l[:, cs] = l[:, cs] * fade + jnp.sum(p, axis=0, keepdims=True)
            m[:, cs] = now
            acc[:, cs] = acc[:, cs] * fade + tn(values, p.astype(BF))

        def block(ref, u):
            return ref[pl.ds(pl.multiple_of(u * KEYS, KEYS), KEYS), :]

        spans = [slice(lo, lo + SPAN) for lo in range(0, rows, SPAN)]
        blocks = (used + KEYS - 1) // KEYS
        for cs in spans:
            s_a[:, cs] = nt(block(k_ref, 0), q_all[cs, :])

        def visit(u, _):
            for now, then, at in ((s_a, s_b, 2 * u), (s_b, s_a, 2 * u + 1)):
                k_next, v_here = block(k_ref, at + 1), block(v_ref, at)
                for cs in spans:
                    then[:, cs] = nt(k_next, q_all[cs, :])
                    absorb(now[:, cs], v_here, cs)
            return 0

        lax.fori_loop(0, blocks // 2, visit, 0)

        @pl.when(lax.rem(blocks, 2) == 1)
        def _():
            v_last = block(v_ref, blocks - 1)
            for cs in spans:
                absorb(s_a[:, cs], v_last, cs)

        extra = (blocks * KEYS - counted).astype(F32)
        first = nt(k_ref[0:8, :], q_all[...])[0:1]
        l[...] = l[...] - extra * jnp.exp(first - m[...])
        for part, kv_ref in enumerate(fresh_refs):
            new_keys, new_values = kv_ref[:, :d], kv_ref[:, d:]
            row = lax.broadcasted_iota(jnp.int32, (fresh, 1), 0)
            side = c if part == 0 else 1 - c
            key_token = z * (4 * t) + (row // t) * (2 * t) + side * t + lax.rem(row, t)
            for cs in spans:
                s = nt(new_keys, q_all[cs, :])
                absorb(jnp.where(key_token <= token[:, cs], s, NEG), new_values, cs)
        top = m[...]
        top_hi = top.astype(BF).astype(F32)
        top_lo = (top - top_hi).astype(BF).astype(F32)
        scale = jnp.exp(top - (top_hi + top_lo))
        den = l[...] * scale
        den_hi = den.astype(BF).astype(F32)
        den_lo = den - den_hi
        numer = (acc[...] * scale).T
        stats[...] = jnp.zeros(stats.shape, F32)
        for i in range(n):
            owner = lax.rem(z + nz - dists[i], nz)
            for h in range(g):
                at = slice((i * g + h) * t, (i * g + h + 1) * t)
                out[:, owner, :, h * d : (h + 1) * d] = numer[at].reshape(n, t // n, d).astype(BF)
                for k, row in enumerate((top_hi, top_lo, den_hi, den_lo)):
                    stats[8 * k + h : 8 * k + h + 1, :] = row[:, at]
            out[:, owner, :, g * d :] = stats[...].T.reshape(n, t // n, 128).astype(BF)

    return pl.pallas_call(
        kernel,
        out_shape=jax.ShapeDtypeStruct((n, n, t // n, width + 128), BF),
        in_specs=[SM] + [VM] * (n + 2 * ns + 2),
        out_specs=VM,
        scratch_shapes=[
            pltpu.VMEM((rows, d), BF),
            pltpu.VMEM((1, rows), F32),
            pltpu.VMEM((1, rows), F32),
            pltpu.VMEM((d, rows), F32),
            pltpu.VMEM((KEYS, rows), F32),
            pltpu.VMEM((KEYS, rows), F32),
            pltpu.VMEM((1, rows), jnp.int32),
            pltpu.VMEM((128, t), F32),
            pltpu.VMEM((room, d), BF),
            pltpu.VMEM((room, d), BF),
        ],
        compiler_params=params(),
        name="attend",
    )(where, *chunks, *keys, *values, *fresh_pair)


def merge(parts, d):
    n, t, width = parts.shape
    g = (width - 128) // d

    def kernel(ins, out):
        stats = [ins[i, :, g * d :].astype(F32) for i in range(n)]
        for h in range(g):
            tops = [s[:, h : h + 1] + s[:, 8 + h : 9 + h] for s in stats]
            dens = [s[:, 16 + h : 17 + h] + s[:, 24 + h : 25 + h] for s in stats]
            top = functools.reduce(jnp.maximum, tops)
            shares = [jnp.exp(a - top) for a in tops]
            den = sum(w * a for w, a in zip(shares, dens))
            num = sum(w * ins[i, :, h * d : (h + 1) * d].astype(F32) for i, w in enumerate(shares))
            out[:, h * d : (h + 1) * d] = (num / den).astype(BF)

    return pl.pallas_call(
        kernel,
        out_shape=jax.ShapeDtypeStruct((t, g * d), BF),
        in_specs=[VM],
        out_specs=VM,
        compiler_params=params(),
        name="merge",
    )(parts)


def project_out(where, contexts, weights, n):
    t, inner = contexts[0].shape
    cols = weights.shape[0]
    part = t // n

    def kernel(where_ref, *refs):
        c_refs, (w_ref, out, tokens) = refs[:4], refs[4:]
        here = 2 * where_ref[1] + where_ref[2]
        for f in range(4):
            tokens[:, f ^ here] = c_refs[f][...].reshape(n, part, inner).astype(F32)
        rows = tokens[...].reshape(4 * t, inner).astype(BF)
        out[...] = nt(rows, w_ref[...]).astype(BF).reshape(n, 4 * part, cols)

    return pl.pallas_call(
        kernel,
        out_shape=jax.ShapeDtypeStruct((n, 4 * part, cols), BF),
        in_specs=[SM] + [VM] * 5,
        out_specs=VM,
        scratch_shapes=[pltpu.VMEM((n, 4, part, inner), F32)],
        compiler_params=params(),
        name="project_out",
    )(where, *contexts, weights)


def sum_heads(parts, n):
    heads, rows, cols = parts.shape
    width = cols // n

    def kernel(p_ref, out):
        total = p_ref[0].astype(F32)
        for i in range(1, heads):
            total = total + p_ref[i].astype(F32)
        for k in range(n):
            out[k] = total[:, k * width : (k + 1) * width].astype(BF)

    return pl.pallas_call(
        kernel,
        out_shape=jax.ShapeDtypeStruct((n, rows, width), BF),
        in_specs=[VM],
        out_specs=VM,
        compiler_params=params(),
        name="sum_heads",
    )(parts)


def per_device(
    hidden,
    norm_gain,
    w_query,
    key_projection_weight,
    value_projection_weight,
    w_out,
    cache_keys,
    earlier_values,
    cache_len,
    stretch_start,
):
    t, model = hidden.shape
    d = cache_keys.shape[2]
    q_cols = w_query.shape[1]
    kv_cols = key_projection_weight.shape[1]
    nz = lax.axis_size("z")
    z, y, c = lax.axis_index("z"), lax.axis_index("y"), lax.axis_index("c")
    where = jnp.stack([z, y, c, jnp.int32(nz)]).astype(jnp.int32)

    cut = norm_cut(hidden, norm_gain, nz)
    x = lax.all_to_all(cut, ("y", "c"), 0, 0, tiled=True).reshape(4 * t, model // 4)
    near = with_length(cache_keys[0], cache_len)

    weights = side_by_side([w_query, key_projection_weight, value_projection_weight])
    links = {1: cut, 2: shift(near, "y", 1), 3: x}
    blocks = ring(weights, "z", links)
    beside, x = links[2], links[3]

    keys = [near, beside, shift(near, "c", 1), shift(beside, "c", 1)]

    keep, send = project(where, x, blocks)
    out_cols, keep = lax.optimization_barrier((w_out.T, keep))
    out_cols = lax.all_gather(out_cols, "z", axis=0, tiled=True)

    near, _ = lax.optimization_barrier((earlier_values[0], x))
    beside, came = lax.optimization_barrier((shift(near, "y", 1), shift(send, "c", 1)))
    values = [near, beside, shift(near, "c", 1), shift(beside, "c", 1)]
    q_near, q_away, kv = sum_cores(where, keep, came, q_cols)
    queries = (q_near + shift(q_away, "y", 1)).astype(BF)
    fresh = (kv + shift(kv, "y", 1)).astype(BF).reshape(2 * t, 2 * kv_cols)
    other = shift(fresh, "c", 1)

    token = lax.axis_index(BLK) * t + jnp.arange(t, dtype=jnp.int32)
    positions = stretch_start[0] + token
    temper = jnp.log(((positions + 1) // 8192).astype(F32) + 1.0) * 0.1 + 1.0
    scaled = (
        lax.optimization_barrier(queries).astype(F32) * (temper * d ** (-0.5))[:, None]
    ).astype(BF)

    chunks = ring(scaled, "z", {nz: scaled})
    partial = attend(where, chunks, list(range(nz)), keys, values, (fresh, other))
    returned = lax.all_to_all(partial, "z", 0, 0, tiled=True)
    context = merge(returned.reshape(nz, t, -1), d)
    context_y = shift(context, "y", 1)
    contexts = [context, shift(context, "c", 1), context_y, shift(context_y, "c", 1)]
    terms = project_out(where, contexts, out_cols, nz)
    shares = lax.all_to_all(terms, "head", 0, 0, tiled=True)
    final = lax.all_to_all(sum_heads(shares, nz), "z", 0, 0, tiled=True)
    final = final.reshape(nz, 4, t // nz, -1).transpose(1, 0, 2, 3)
    return final.reshape(4 * t, -1)


def solution(mesh):
    finer = Mesh(mesh.devices.reshape(8, 2, 2, mesh.shape["head"]), ("z", "y", "c", "head"))
    return jax.shard_map(
        per_device,
        mesh=finer,
        in_specs=(
            P(BLK, None),
            P(),
            P(BLK, "head"),
            P(BLK, "head"),
            P(BLK, "head"),
            P("head", BLK),
            P("head", BLK, None),
            P("head", BLK, None),
            P(BLK),
            P(),
        ),
        out_specs=P("head", BLK),
        check_vma=False,
    )
```
